256 devices in a mesh: image: 2 (over core), dom: 128 (over y, z, x).
Axes of the slice: x: 4, y: 4, z: 8, core: 2. Of those that a mesh axis runs over, the one named last changes fastest.
Arguments:
- positions: float32 [3, 131072], P(None, 'dom'), may hold values from 0 to 1
- mode: float32 [3, 131072], P(None, 'dom'), may hold values from -6 to 6
- features: float32 [64, 131072], P(None, 'dom'), may hold values from -6 to 6
- neighbours: int32 [12, 131072], P(None, 'dom'), may hold values from -1 to 2047, as said below
- counts: int32 [128], P('dom'), may hold values from 512 to 1024, as said below
- send_index: int32 [2, 65536], P(None, 'dom'), may hold values from 0 to 1023, as said below
- w_filter_in: float32 [32, 64], replicated, may hold values from -1 to 1
- b_filter: float32 [64], replicated, may hold values from -4 to 4
- w_filter_out: float32 [64, 64], replicated, may hold values from -0.75 to 0.75
- w_project: float32 [64, 64], replicated, may hold values from -0.75 to 0.75
- w_update_in: float32 [64, 64], replicated, may hold values from -0.75 to 0.75
- b_update: float32 [64], replicated, may hold values from -4 to 4
- w_update_out: float32 [64, 64], replicated, may hold values from -0.75 to 0.75
- w_readout: float32 [64, 64], replicated, may hold values from -0.75 to 0.75
- w_energy: float32 [64], replicated, may hold values from -0.75 to 0.75
Outputs:
- forces: float32 [2, 3, 131072], P('image', None, 'dom')
- rot_force: float32 [3, 2, 65536], P(None, 'image', 'dom')
- new_mode: float32 [3, 2, 65536], P(None, 'image', 'dom')
- curvature: float32 [1], replicated
The draws below stay inside these ranges and needn't reach their ends.
Inputs may be any that keep to these rules, and one draw needn't show every extreme that they name: `counts`: some domain holds exactly 1024 atoms. `neighbours`: for slot i of a domain with c atoms: -1 marks an empty slot; every slot of an atom i >= c is empty; otherwise an entry is an own atom 0 to c - 1 other than i, or 1024 + h for the h-th left rim atom, or 1536 + h for the h-th right rim atom (h < 512). Each atom below c fills its first 6 to 12 slots. `send_index`: columns d * 512 to (d + 1) * 512 - 1 name atoms of domain d below its count, repeats allowed; row 0 those sent to the lower neighbour, row 1 those sent to the upper one.
All inputs are finite; a program needn't handle non-finite values.
Results may differ from the reference program's by a relative error of at most 0.0003.
Values sent between devices are 32-bit elements; how exact they have to be, the bound alone decides.
A program may use at most 64 MiB of HBM per device.

```python
import jax
import jax.numpy as jnp
from jax import lax

CH = 64
RBF = 32
NBR = 12
A_MAX = 1024
H = 512
ATOMS = 131072


def domain_counts(key):
    base = jax.random.fold_in(key, 7)
    first, second = jax.random.split(base)
    domains = ATOMS // A_MAX
    drawn = jax.random.randint(first, (domains,), A_MAX // 2, A_MAX + 1)
    full_domain = jax.random.randint(second, (), 0, domains)
    return jnp.where(jnp.arange(domains) == full_domain, A_MAX, drawn).astype(jnp.int32)


def draw_counts(key, part):
    return domain_counts(key)


def draw_neighbours(key, part):
    counts = domain_counts(key)
    limits = jnp.repeat(counts, A_MAX)
    atom = jnp.arange(ATOMS, dtype=jnp.int32) % A_MAX
    base = jax.random.fold_in(key, 13)
    key_deg, key_local, key_rim, key_pick = jax.random.split(base, 4)
    degree = jax.random.randint(key_deg, (ATOMS,), 6, NBR + 1)
    degree = jnp.where(atom == 0, NBR, degree)
    local = jax.random.randint(key_local, (NBR, ATOMS), 0, limits[None, :] - 1)
    local = jnp.where(local >= atom[None, :], local + 1, local)
    rim_pick = A_MAX + jax.random.randint(key_rim, (NBR, ATOMS), 0, 2 * H)
    choose = jax.random.randint(key_pick, (NBR, ATOMS), 0, 2)
    values = jnp.where(choose == 0, local, rim_pick)
    slot = jnp.arange(NBR, dtype=jnp.int32)[:, None]
    values = jnp.where((atom[None, :] == 0) & (slot == 0), 2 * A_MAX - 1, values)
    filled = (slot < degree[None, :]) & (atom[None, :] < limits[None, :])
    return jnp.where(filled, values, -1).astype(jnp.int32)


def draw_send_index(key, part):
    counts = domain_counts(key)
    domains = ATOMS // A_MAX
    limits = jnp.repeat(counts, H)
    base = jax.random.fold_in(key, 19)
    values = jax.random.randint(base, (2, H * domains), 0, limits[None, :])
    place = jnp.arange(H * domains, dtype=jnp.int32) % H
    row = jnp.arange(2, dtype=jnp.int32)[:, None]
    values = jnp.where((row == 1) & (place[None, :] == 0), limits[None, :] - 1, values)
    return values.astype(jnp.int32)


def steps_of(own_key, dims, cuts, smallest, top_value):
    def one(axis_at, shards_of):
        steps = jax.random.uniform(jax.random.fold_in(jax.random.fold_in(own_key, 6), axis_at), (shards_of,), jnp.float32, smallest / len(cuts), top_value / len(cuts))
        return jnp.repeat(jnp.exp(steps), dims[axis_at] // shards_of).reshape((-1,) + (1,) * (len(dims) - axis_at - 1))

    gain = one(*cuts[0])
    for cut in cuts[1:]:
        gain = gain * one(*cut)
    return gain


def noise(key, dims, spread, bound, cuts=(), held_as=jnp.bfloat16):
    values = jax.random.normal(key, dims, jnp.float32) * spread
    if len(cuts) > 0:
        values = steps_of(key, dims, cuts, -0.22, 0.18) * values
    return jnp.clip(values, min=-bound, max=bound).astype(held_as)


def setup_inputs(seed: int = 0) -> dict:
    streams_of = jax.random.split(jax.random.key(seed), 16)
    return {
        "positions": jnp.clip(1.0 * jax.random.uniform(streams_of[0], (3, ATOMS), jnp.float32) ** steps_of(streams_of[0], (3, ATOMS), ((1, 128),), -0.2, 0.2), 0.0, 1.0),
        "mode": noise(streams_of[1], (3, ATOMS), 1.0, 6.0, ((1, 128),), jnp.float32),
        "features": noise(streams_of[2], (CH, ATOMS), 1.0, 6.0, ((1, 128),), jnp.float32),
        "neighbours": draw_neighbours(jax.random.fold_in(streams_of[15], 71), 0),
        "counts": draw_counts(jax.random.fold_in(streams_of[15], 71), 0),
        "send_index": draw_send_index(jax.random.fold_in(streams_of[15], 71), 0),
        "w_filter_in": noise(streams_of[6], (RBF, CH), RBF ** -0.5, 1.0, (), jnp.float32),
        "b_filter": noise(streams_of[7], (CH,), 1.0, 4.0, (), jnp.float32),
        "w_filter_out": noise(streams_of[8], (CH, CH), CH ** -0.5, 0.75, (), jnp.float32),
        "w_project": noise(streams_of[9], (CH, CH), CH ** -0.5, 0.75, (), jnp.float32),
        "w_update_in": noise(streams_of[10], (CH, CH), CH ** -0.5, 0.75, (), jnp.float32),
        "b_update": noise(streams_of[11], (CH,), 1.0, 4.0, (), jnp.float32),
        "w_update_out": noise(streams_of[12], (CH, CH), CH ** -0.5, 0.75, (), jnp.float32),
        "w_readout": noise(streams_of[13], (CH, CH), CH ** -0.5, 0.75, (), jnp.float32),
        "w_energy": noise(streams_of[14], (CH,), CH ** -0.5, 0.75, (), jnp.float32),
    }


dimer_step = 0.05
turn_rate = 0.5

def local_energy(pos_ext, feat_ext, neighbour_rows, valid, w_filter_in, b_filter, w_filter_out, w_project, w_update_in, b_update, w_update_out, w_readout, w_energy):
    highest = lax.Precision.HIGHEST
    atom_slots = neighbour_rows.shape[1]
    basis_count = w_filter_in.shape[0]
    own_positions = pos_ext[:, :atom_slots]
    projected = jnp.dot(w_project.T, feat_ext, precision=highest, preferred_element_type=jnp.float32)
    centers = 2.5 * jnp.arange(basis_count, dtype=jnp.float32) / (basis_count - 1)
    sharpness = 0.25 * ((basis_count - 1) / 2.5) ** 2

    def one_slot(summed, slot_row):
        target = jnp.maximum(slot_row, 0)
        filled = (slot_row >= 0).astype(jnp.float32)
        offsets = pos_ext[:, target] - own_positions
        distance = jnp.sqrt(lax.optimization_barrier(jnp.sum(offsets * offsets, axis=0)) + 0.01)
        basis = jnp.exp(-sharpness * (distance[None, :] - centers[:, None]) ** 2)
        hidden = jax.nn.silu(jnp.dot(w_filter_in.T, basis, precision=highest, preferred_element_type=jnp.float32) + b_filter[:, None])
        filt = jnp.dot(w_filter_out.T, hidden, precision=highest, preferred_element_type=jnp.float32)
        return (summed + filt * projected[:, target] * filled[None, :], None)
    start = jnp.zeros((w_project.shape[1], atom_slots), jnp.float32)
    summed, _ = lax.scan(jax.checkpoint(one_slot), start, neighbour_rows)
    inner = jax.nn.silu(jnp.dot(w_update_in.T, summed, precision=highest, preferred_element_type=jnp.float32) + b_update[:, None])
    updated = feat_ext[:, :atom_slots] + jnp.dot(w_update_out.T, inner, precision=highest, preferred_element_type=jnp.float32)
    readout = jax.nn.silu(jnp.dot(w_readout.T, updated, precision=highest, preferred_element_type=jnp.float32))
    atom_energy = jnp.dot(w_energy, readout, precision=highest, preferred_element_type=jnp.float32)
    return jnp.sum(valid * atom_energy)

def reference(positions, mode, features, neighbours, counts, send_index, w_filter_in, b_filter, w_filter_out, w_project, w_update_in, b_update, w_update_out, w_readout, w_energy):
    domains = counts.shape[0]
    slots = positions.shape[1] // domains
    rim_width = send_index.shape[1] // domains
    valid_grid = (jnp.arange(slots, dtype=jnp.int32)[None, :] < counts[:, None]).astype(jnp.float32)
    valid = valid_grid.reshape(-1)
    masked = mode * valid[None, :]
    total = 3.0 * positions.shape[1]
    unit_mode = masked * jnp.sqrt(total / jnp.sum(masked * masked))

    def per_domain(values):
        return values.reshape(values.shape[0], domains, slots).transpose(1, 0, 2)
    send_domain = send_index.reshape(2, domains, rim_width).transpose(1, 0, 2)

    def blocks_of(values):
        return jax.vmap(lambda part, picks: part[:, picks.reshape(-1)])(values, send_domain)

    def rims(blocks):
        return (jnp.roll(blocks, 1, 0)[:, :, rim_width:], jnp.roll(blocks, -1, 0)[:, :, :rim_width])
    feat_domain = per_domain(features)
    neighbour_domain = per_domain(neighbours)
    feat_left, feat_right = rims(blocks_of(feat_domain))
    shift_x = jnp.array([1.0, 0.0, 0.0], jnp.float32)[:, None]
    weights = (w_filter_in, b_filter, w_filter_out, w_project, w_update_in, b_update, w_update_out, w_readout, w_energy)
    image_forces = []
    for image in range(2):
        sign = 1.0 - 2.0 * image
        shifted = positions + sign * dimer_step * unit_mode
        pos_domain = per_domain(shifted)
        pos_left, pos_right = rims(blocks_of(pos_domain))

        def one_domain(pieces):
            own_pos, left_pos, right_pos, own_feat, left_feat, right_feat, rows, valid_row = pieces
            pos_ext = jnp.concatenate([own_pos, left_pos - shift_x, right_pos + shift_x], axis=1)
            feat_ext = jnp.concatenate([own_feat, left_feat, right_feat], axis=1)
            return jax.grad(local_energy)(pos_ext, feat_ext, rows, valid_row, *weights)
        grads = lax.map(one_domain, (pos_domain, pos_left, pos_right, feat_domain, feat_left, feat_right, neighbour_domain, valid_grid))
        from_left = jnp.roll(grads[:, :, slots + rim_width:], 1, 0)
        from_right = jnp.roll(grads[:, :, slots:slots + rim_width], -1, 0)
        returned = jnp.concatenate([from_left, from_right], axis=2)
        own = jax.vmap(lambda grad_own, picks, extra: grad_own.at[:, picks.reshape(-1)].add(extra))(grads[:, :, :slots], send_domain, returned)
        image_forces.append(-own.transpose(1, 0, 2).reshape(3, -1))
    difference = (image_forces[0] - image_forces[1]) / (2.0 * dimer_step)
    projection = jnp.sum(difference * unit_mode)
    rot_full = difference - projection / total * unit_mode
    curvature = jnp.reshape(-projection / total, (1,))
    moved = unit_mode + turn_rate * rot_full
    mode_full = moved * jnp.sqrt(total / jnp.sum(moved * moved))
    forces = jnp.stack(image_forces, axis=0)

    def halves(values):
        return values.reshape(3, domains, 2, slots // 2).transpose(0, 2, 1, 3).reshape(3, 2, domains * (slots // 2))
    return (forces, halves(rot_full), halves(mode_full), curvature)
```

```python
import functools

import jax
import jax.numpy as jnp
from jax import lax
from jax.experimental import pallas as pl
from jax.experimental.pallas import tpu as pltpu
from jax.sharding import PartitionSpec as P

f32 = jnp.float32
bf = jnp.bfloat16
CH = 64
RBF = 32
NBR = 12
A = 1024
H = 512
LO = 256
STEP = 0.05
TURN = 0.5
X, Y, Z = 4, 4, 8
G1, G2 = X * Y, Z
DOM = X * Y * Z
TOTAL = 3.0 * DOM * A
MESH = pl.DeviceIdType.MESH


def split(x):
    hi = x.astype(bf)
    return hi, (x - hi.astype(f32)).astype(bf)

def wcat(w):
    hi, lo = split(w)
    return jnp.concatenate([hi, lo, hi], axis=1)

def dot3(wc, x):
    hi, lo = split(x)
    return jnp.dot(wc, jnp.concatenate([hi, hi, lo], axis=0), preferred_element_type=f32)

def column(row_ref):
    return jnp.broadcast_to(row_ref[...], (128, row_ref.shape[1])).T

def tiled(col, L):
    return jnp.concatenate([col] * (L // 128), axis=1)

def sig(x):
    return 0.5 * jnp.tanh(0.5 * x) + 0.5

def stage_tab(proj, tab):
    for h in range(8):
        hi, lo = split(proj[:, h*LO:(h+1)*LO])
        tab[h*64:(h+1)*64, 0:LO] = hi
        tab[h*64:(h+1)*64, LO:2*LO] = lo

def stage_a(k, nbr, tab, onehot, pt, L=256):
    row = nbr[pl.ds(k, 1), :]
    for l in range(0, A, L):
        idx = row[:, l:l+L]
        lo = idx & (LO-1); hi = idx >> 8
        O = jnp.where(lax.broadcasted_iota(jnp.int32, (LO, L), 0) == lo, 1.0, 0.0).astype(bf)
        onehot[k, :, l:l+L] = O
        G = jnp.dot(tab[...], jnp.concatenate([O, O], axis=0), preferred_element_type=f32)
        acc = jnp.zeros((64, L), f32)
        for h in range(8):
            acc = jnp.where(hi == h, G[h*64:h*64+64], acc)
        pt[k, :, l:l+L] = acc

def stage_b(k, nbr, pos8, w1, w2, bcol, pt, summed, od, L=256):
    row = nbr[pl.ds(k, 1), :]
    step = 2.5 / (RBF - 1)
    g = 0.25 * ((RBF - 1) / 2.5) ** 2
    cen = lax.broadcasted_iota(jnp.int32, (RBF, L), 0).astype(f32) * 2.5 / (RBF - 1)
    bl = tiled(bcol[...], L)
    for l in range(0, A, L):
        parts = []
        for m in range(l, l+L, 128):
            idx = row[:, m:m+128]
            lo = jnp.broadcast_to(idx & 127, (8, 128)); hi = jnp.broadcast_to(idx >> 7, (8, 128))
            acc = jnp.zeros((8, 128), f32)
            for h in range(16):
                v = jnp.take_along_axis(pos8[:, h*128:h*128+128], lo, axis=1)
                acc = jnp.where(hi == h, v, acc)
            parts.append(acc)
        off = jnp.concatenate(parts, axis=1) - pos8[:, l:l+L]
        d2 = jnp.sum(off * off, axis=0, keepdims=True) + 0.01
        d = jnp.sqrt(d2)
        od[k, :, l:l+L] = off / d
        t = d - cen
        basis = jnp.exp(-g * (t * t))
        bp = basis * ((-2.0 * g) * t)
        pq = dot3(w1[...], jnp.concatenate([basis, bp], axis=1))
        pre = pq[:, :L] + bl
        q = pq[:, L:]
        s = sig(pre)
        hdn = pre * s
        z = (s + hdn * (1.0 - s)) * q
        ff = dot3(w2[...], jnp.concatenate([hdn, z], axis=1))
        gt = pt[k, :, l:l+L]
        summed[:, l:l+L] += ff[:, :L] * gt
        pt[k, :, l:l+L] = ff[:, L:] * gt

def stage_c(summed, feat, cnt, wui, wuit, wuo, wuot, wr, wrt, bucol, wecol, L=512):
    for l in range(0, A, L):
        pre = dot3(wuit[...], summed[:, l:l+L]) + tiled(bucol[...], L)
        s = sig(pre)
        inner = pre * s
        upd = feat[:, l:l+L] + dot3(wuot[...], inner)
        r = dot3(wrt[...], upd)
        sr = sig(r)
        valid = lax.broadcasted_iota(jnp.int32, (CH, L), 1) + l < cnt
        dr = jnp.where(valid, tiled(wecol[...], L) * (sr + r * sr * (1.0 - sr)), 0.0)
        du = dot3(wr[...], dr)
        di = dot3(wuo[...], du)
        dp = di * (s + inner * (1.0 - s))
        summed[:, l:l+L] = dot3(wui[...], dp)

def stage_d(k, nbr, onehot, pt, od, dsum, own, sc):
    row = nbr[pl.ds(k, 1), :]
    hi = row >> 8
    dd = jnp.sum(dsum[...] * pt[k], axis=0, keepdims=True)
    D = od[k] * dd
    own[...] -= D
    Dh = D.astype(bf).astype(f32)
    Dl = D - Dh
    D8 = Dh + pltpu.roll(Dl, 3, axis=0)
    Gm = jnp.concatenate([jnp.where(hi == h, D8, 0.0) for h in range(8)], axis=0).astype(bf)
    sc[...] += lax.dot_general(Gm, onehot[k], (((1,), (1,)), ((), ())), preferred_element_type=f32)

def kernel(stop, pos8, proj, nbr, cnt_ref, feat, wfi, bf_, wfo, wui_, bu, wuo_, wr_, we, out,
           tab, onehot, pt, summed, od, own, sc, w1, w2, bcol, bucol, wecol, wui, wuit, wuo, wuot, wr, wrt):
    cnt = cnt_ref[0]
    w1[...] = wcat(wfi[...].T); w2[...] = wcat(wfo[...].T)
    wui[...] = wcat(wui_[...]); wuit[...] = wcat(wui_[...].T)
    wuo[...] = wcat(wuo_[...]); wuot[...] = wcat(wuo_[...].T)
    wr[...] = wcat(wr_[...]); wrt[...] = wcat(wr_[...].T)
    bcol[...] = column(bf_); bucol[...] = column(bu); wecol[...] = column(we)
    stage_tab(proj, tab)
    out[...] = jnp.zeros_like(out)
    summed[...] = jnp.zeros_like(summed)
    own[...] = jnp.zeros_like(own)
    sc[...] = jnp.zeros_like(sc)
    if stop < 1: return
    def la(k, c):
        stage_a(k, nbr, tab, onehot, pt); return c
    lax.fori_loop(0, NBR, la, 0)
    if stop < 2: return
    def lb(k, c):
        stage_b(k, nbr, pos8, w1, w2, bcol, pt, summed, od); return c
    lax.fori_loop(0, NBR, lb, 0)
    if stop < 3: return
    stage_c(summed, feat, cnt, wui, wuit, wuo, wuot, wr, wrt, bucol, wecol)
    if stop < 4: return
    def ld(k, c):
        stage_d(k, nbr, onehot, pt, od, summed, own, sc); return c
    lax.fori_loop(0, NBR, ld, 0)
    for h in range(8):
        v = sc[h*8:h*8+8, :]
        v = v + pltpu.roll(v, 5, axis=0)
        if h < 4:
            v = v + own[:, h*LO:(h+1)*LO]
        out[:, h*LO:(h+1)*LO] = v

def make(stop=9):
    V = lambda *s, dt=f32: pltpu.VMEM(s, dt)
    vm = pl.BlockSpec(memory_space=pltpu.VMEM)
    return pl.pallas_call(functools.partial(kernel, stop), out_shape=jax.ShapeDtypeStruct((8, 2048), f32),
        in_specs=[vm, vm, vm, pl.BlockSpec(memory_space=pltpu.SMEM)] + [vm]*9, out_specs=vm,
        scratch_shapes=[V(512,512,dt=bf), V(12,256,1024,dt=bf), V(12,64,1024), V(64,1024), V(12,8,1024), V(8,1024), V(64,256),
            V(64,96,dt=bf), V(64,192,dt=bf), V(64,128), V(64,128), V(64,128)] + [V(64,192,dt=bf)]*6, name=f"k2s{stop}")


class Place:
    def __init__(self):
        self.image = lax.axis_index("image")
        self.dom = lax.axis_index("dom")
        self.x = self.dom % X
        self.z = (self.dom // X) % Z
        self.y = self.dom // (X * Z)
        self.slot1 = self.y * X + self.x
        self.up = (self.image, (self.dom + 1) % DOM)
        self.down = (self.image, (self.dom + DOM - 1) % DOM)
        self.partner = (1 - self.image, self.dom)

    def peer1(self, o):
        s = (self.slot1 + o) % G1
        return (self.image, (s // X) * (X * Z) + self.z * X + s % X)

    def peer2(self, o):
        return (self.image, self.y * (X * Z) + ((self.z + o) % Z) * X + self.x)


def greet(pos, extra):
    barrier = pltpu.get_barrier_semaphore()
    peers = [pos.peer1(o) for o in range(1, G1)] + [pos.peer2(o) for o in range(1, G2)] + extra
    for peer in peers:
        pl.semaphore_signal(barrier, inc=1, device_id=peer, device_id_type=MESH)
    return barrier, len(peers)


def spread(src, dst, slot, count, peer_of, ssem, rsem):
    copies = []
    for o in range(1, count):
        copy = pltpu.make_async_remote_copy(
            src_ref=src.at[0], dst_ref=dst.at[slot], send_sem=ssem.at[o], recv_sem=rsem.at[slot],
            device_id=peer_of(o), device_id_type=MESH)
        copy.start()
        copies.append(copy)
    return copies


def gather_wait(dst, slot, count, rsem, src, ssem, peer_of):
    for o in range(1, count):
        other = (slot + o) % count
        pltpu.make_async_remote_copy(
            src_ref=src.at[0], dst_ref=dst.at[other], send_sem=ssem.at[o], recv_sem=rsem.at[other],
            device_id=peer_of(o), device_id_type=MESH).wait_recv()


def shift_of(side):
    return jnp.where(lax.broadcasted_iota(jnp.int32, (8, H), 0) == 0, side, 0.0)


def kernel1(pos_ref, mode_ref, feat, cnt_ref, send_ref, wp_ref, pos8, proj, unit,
            tab, pm, rim, left, right, src1, red1, src2, red2,
            hs, hr, s1, r1, s2, r2):
    pos = Place()
    barrier, count = greet(pos, [pos.up, pos.down])
    valid = lax.broadcasted_iota(jnp.int32, (3, A), 1) < cnt_ref[0]
    masked = jnp.where(valid, mode_ref[...], 0.0)
    part = jnp.sum(jnp.sum(masked * masked, axis=1, keepdims=True), axis=0, keepdims=True)
    src1[0] = jnp.broadcast_to(part, (1, 128))
    red1[pl.ds(pos.slot1, 1)] = jnp.broadcast_to(part, (1, 1, 128))
    pm[...] = jnp.concatenate([pos_ref[...], masked, jnp.zeros((2, A), f32)], axis=0)
    wpt = wcat(wp_ref[...].T)
    for h in range(4):
        own = dot3(wpt, feat[:, h * LO:(h + 1) * LO])
        proj[:, h * LO:(h + 1) * LO] = own
        hi, lo = split(own)
        tab[h * 64:(h + 1) * 64, 0:LO] = hi
        tab[h * 64:(h + 1) * 64, LO:2 * LO] = lo
    for side in range(2):
        row = send_ref[side:side + 1, :]
        for l in range(0, H, 256):
            idx = row[:, l:l + 256]
            lo, hi = idx & (LO - 1), idx >> 8
            O = jnp.where(lax.broadcasted_iota(jnp.int32, (LO, 256), 0) == lo, 1.0, 0.0).astype(bf)
            G = jnp.dot(tab[...], jnp.concatenate([O, O], axis=0), preferred_element_type=f32)
            acc = jnp.zeros((64, 256), f32)
            for h in range(4):
                acc = jnp.where(hi == h, G[h * 64:h * 64 + 64], acc)
            rim[side, 0:64, l:l + 256] = acc
        for l in range(0, H, 128):
            idx = row[:, l:l + 128]
            lo = jnp.broadcast_to(idx & 127, (8, 128))
            hi = jnp.broadcast_to(idx >> 7, (8, 128))
            acc = jnp.zeros((8, 128), f32)
            for h in range(8):
                v = jnp.take_along_axis(pm[:, h * 128:h * 128 + 128], lo, axis=1)
                acc = jnp.where(hi == h, v, acc)
            rim[side, 64:72, l:l + 128] = acc
    pl.semaphore_wait(barrier, count)
    c1 = spread(src1, red1, pos.slot1, G1, pos.peer1, s1, r1)
    low = pltpu.make_async_remote_copy(
        src_ref=rim.at[0], dst_ref=right, send_sem=hs.at[0], recv_sem=hr.at[0],
        device_id=pos.down, device_id_type=MESH)
    high = pltpu.make_async_remote_copy(
        src_ref=rim.at[1], dst_ref=left, send_sem=hs.at[1], recv_sem=hr.at[1],
        device_id=pos.up, device_id_type=MESH)
    low.start()
    high.start()
    gather_wait(red1, pos.slot1, G1, r1, src1, s1, pos.peer1)
    part = red1[0]
    for i in range(1, G1):
        part = part + red1[i]
    src2[0] = part
    red2[pl.ds(pos.z, 1)] = part[None]
    c2 = spread(src2, red2, pos.z, G2, pos.peer2, s2, r2)
    gather_wait(red2, pos.z, G2, r2, src2, s2, pos.peer2)
    part = red2[0]
    for i in range(1, G2):
        part = part + red2[i]
    scale = jnp.sqrt(TOTAL / part[:, 0:1])
    moves = (1.0 - 2.0 * pos.image.astype(f32)) * STEP
    zero5 = jnp.zeros((5, A), f32)
    u = pm[3:6, :] * scale
    unit[...] = jnp.concatenate([u, zero5], axis=0)
    pos8[:, 0:A] = jnp.concatenate([pm[0:3, :] + moves * u, zero5], axis=0)
    low.wait_recv()
    high.wait_recv()
    for buf, at, side in ((left, A, -1.0), (right, A + H, 1.0)):
        proj[:, at:at + H] = buf[0:64, :]
        p = buf[64:67, :] + moves * (buf[67:70, :] * scale)
        pos8[:, at:at + H] = jnp.concatenate([p, jnp.zeros((5, H), f32)], axis=0) + shift_of(side)
    for copy in c1 + c2 + [low, high]:
        copy.wait_send()


def kernel3(grad, unit, send_ref, forces, rot_out, mode_out, curv,
            extra, mine, theirs, src1, red1, src2, red2,
            hs, hr, ps, pr, s1, r1, s2, r2):
    pos = Place()
    barrier, count = greet(pos, [pos.up, pos.down, pos.partner])
    pl.semaphore_wait(barrier, count)
    up = pltpu.make_async_remote_copy(
        src_ref=grad.at[:, A + H:A + 2 * H], dst_ref=extra.at[:, 0:H], send_sem=hs.at[0], recv_sem=hr.at[0],
        device_id=pos.up, device_id_type=MESH)
    down = pltpu.make_async_remote_copy(
        src_ref=grad.at[:, A:A + H], dst_ref=extra.at[:, H:2 * H], send_sem=hs.at[1], recv_sem=hr.at[1],
        device_id=pos.down, device_id_type=MESH)
    up.start()
    down.start()
    row = jnp.concatenate([send_ref[0:1, :], send_ref[1:2, :]], axis=1)
    lo, hi = row & (LO - 1), row >> 8
    O = jnp.where(lax.broadcasted_iota(jnp.int32, (LO, A), 0) == lo, 1.0, 0.0).astype(bf)
    up.wait_recv()
    down.wait_recv()
    keep = lax.broadcasted_iota(jnp.int32, (8, A), 0) < 3
    D = jnp.where(keep, extra[...], 0.0)
    Dh = D.astype(bf).astype(f32)
    D8 = Dh + pltpu.roll(D - Dh, 3, axis=0)
    Gm = jnp.concatenate([jnp.where(hi == h, D8, 0.0) for h in range(4)], axis=0).astype(bf)
    S = lax.dot_general(Gm, O, (((1,), (1,)), ((), ())), preferred_element_type=f32)
    for h in range(4):
        v = S[h * 8:h * 8 + 8, :]
        v = v + pltpu.roll(v, 5, axis=0) + grad[:, h * LO:(h + 1) * LO]
        mine[:, h * LO:(h + 1) * LO] = jnp.where(keep[:, 0:LO], -v, 0.0)
    swap = pltpu.make_async_remote_copy(
        src_ref=mine, dst_ref=theirs, send_sem=ps.at[0], recv_sem=pr.at[0],
        device_id=pos.partner, device_id_type=MESH)
    swap.start()
    forces[0] = mine[0:3, :]
    swap.wait_recv()
    sign = 1.0 - 2.0 * pos.image.astype(f32)
    diff = sign * (mine[...] - theirs[...]) / (2.0 * STEP)
    u = unit[...]

    def total(v):
        return jnp.sum(jnp.sum(v, axis=1, keepdims=True), axis=0, keepdims=True)

    def ratio(p, m):
        return jnp.where(m > 0.0, p / jnp.where(m > 0.0, m, 1.0), 0.0)

    lane = lax.broadcasted_iota(jnp.int32, (1, 128), 1)

    def row_of(p, m, r):
        return jnp.where(lane == 0, p, jnp.where(lane == 1, m, r))

    def merge(ref, n):
        rows = [ref[i] for i in range(n)]
        ps_, ms_, rs_ = [[v[:, j:j + 1] for v in rows] for j in range(3)]
        p, m, r = sum(ps_[1:], ps_[0]), sum(ms_[1:], ms_[0]), sum(rs_[1:], rs_[0])
        qs_ = [ratio(a, b) for a, b in zip(ps_, ms_)]
        return p, m, r, qs_, ms_

    p = total(diff * u)
    m = total(u * u)
    rest = diff - ratio(p, m) * u
    mine_row = row_of(p, m, total(rest * rest))
    src1[0] = mine_row
    red1[pl.ds(pos.slot1, 1)] = mine_row[None]
    c1 = spread(src1, red1, pos.slot1, G1, pos.peer1, s1, r1)
    gather_wait(red1, pos.slot1, G1, r1, src1, s1, pos.peer1)
    p, m, r, qs_, ms_ = merge(red1, G1)
    q = ratio(p, m)
    for a, b in zip(qs_, ms_):
        r = r + (a - q) * (a - q) * b
    mine_row = row_of(p, m, r)
    src2[0] = mine_row
    red2[pl.ds(pos.z, 1)] = mine_row[None]
    c2 = spread(src2, red2, pos.z, G2, pos.peer2, s2, r2)
    gather_wait(red2, pos.z, G2, r2, src2, s2, pos.peer2)
    p, m, r, qs_, ms_ = merge(red2, G2)
    slope = p / TOTAL
    norm = (TURN * TURN) * r
    for a, b in zip(qs_, ms_):
        f = 1.0 + TURN * (a - slope)
        norm = norm + f * f * b
    curv[...] = jnp.broadcast_to(-slope, curv.shape)
    rot = diff - slope * u
    moved = (u + TURN * rot) * jnp.sqrt(TOTAL / norm)
    first = pos.image == 0
    for i in range(3):
        rot_out[i] = jnp.where(first, rot[i:i + 1, 0:H], rot[i:i + 1, H:A])
        mode_out[i] = jnp.where(first, moved[i:i + 1, 0:H], moved[i:i + 1, H:A])
    for copy in c1 + c2 + [up, down, swap]:
        copy.wait_send()


def local(positions, mode, features, neighbours, counts, send_index, w_filter_in, b_filter, w_filter_out,
          w_project, w_update_in, b_update, w_update_out, w_readout, w_energy):
    vm = pl.BlockSpec(memory_space=pltpu.VMEM)
    sm = pl.BlockSpec(memory_space=pltpu.SMEM)
    S = jax.ShapeDtypeStruct

    def V(*s, dt=f32):
        return pltpu.VMEM(s, dt)

    dma = pltpu.SemaphoreType.DMA
    reds = [V(1, 1, 128), V(G1, 1, 128), V(1, 1, 128), V(G2, 1, 128)]
    sems = [dma((G1,)), dma((G1,)), dma((G2,)), dma((G2,))]
    pos8, proj, unit = pl.pallas_call(
        kernel1, out_shape=(S((8, 2 * A), f32), S((CH, 2 * A), f32), S((8, A), f32)),
        in_specs=[vm, vm, vm, sm, vm, vm], out_specs=(vm, vm, vm),
        scratch_shapes=[V(256, 512, dt=bf), V(8, A), V(2, 72, H), V(72, H), V(72, H)] + reds + [dma((2,)), dma((2,))] + sems,
        compiler_params=pltpu.CompilerParams(collective_id=0, has_side_effects=True),
    )(positions, mode, features, counts, send_index, w_project)
    grad = make()(pos8, proj, neighbours, counts, features, w_filter_in, b_filter[None], w_filter_out, w_update_in,
                  b_update[None], w_update_out, w_readout, w_energy[None])
    forces, rot, new_mode, curv = pl.pallas_call(
        kernel3, out_shape=(S((1, 3, A), f32), S((3, 1, H), f32), S((3, 1, H), f32), S((1, 1), f32)),
        in_specs=[vm, vm, vm], out_specs=(vm, vm, vm, vm),
        scratch_shapes=[V(8, A), V(8, A), V(8, A)] + reds + [dma((2,)), dma((2,)), dma((1,)), dma((1,))] + sems,
        compiler_params=pltpu.CompilerParams(collective_id=1, has_side_effects=True),
    )(grad, unit, send_index)
    return (forces, rot, new_mode, curv.reshape(1))


def solution(mesh):
    col = P(None, "dom")
    in_specs = (col, col, col, col, P("dom"), col) + (P(),) * 9
    out_specs = (P("image", None, "dom"), P(None, "image", "dom"), P(None, "image", "dom"), P())
    return jax.shard_map(local, mesh=mesh, in_specs=in_specs, out_specs=out_specs, check_vma=False)
```

```python
import functools

import jax
import jax.numpy as jnp
from jax import lax
from jax.experimental import pallas as pl
from jax.experimental.pallas import tpu as pltpu
from jax.sharding import PartitionSpec as P

f32 = jnp.float32
bf = jnp.bfloat16
CH = 64
RBF = 32
NBR = 12
A = 1024
H = 512
LO = 256
STEP = 0.05
TURN = 0.5
X, Y, Z = 4, 4, 8
G1, G2 = X * Y, Z
DOM = X * Y * Z
TOTAL = 3.0 * DOM * A
MESH = pl.DeviceIdType.MESH


def split(x):
    hi = x.astype(bf)
    return hi, (x - hi.astype(f32)).astype(bf)

def wcat(w):
    hi, lo = split(w)
    return jnp.concatenate([hi, lo, hi], axis=1)

def dot3(wc, x):
    hi, lo = split(x)
    return jnp.dot(wc, jnp.concatenate([hi, hi, lo], axis=0), preferred_element_type=f32)

def column(row_ref):
    return jnp.broadcast_to(row_ref[...], (128, row_ref.shape[1])).T

def tiled(col, L):
    return jnp.concatenate([col] * (L // 128), axis=1)

def sig(x):
    return 0.5 * jnp.tanh(0.5 * x) + 0.5

def stage_c(summed, feat, cnt, wui, wuit, wuo, wuot, wr, wrt, bucol, wecol, L=512):
    for l in range(0, A, L):
        pre = dot3(wuit[...], summed[:, l:l+L]) + tiled(bucol[...], L)
        s = sig(pre)
        inner = pre * s
        upd = feat[:, l:l+L] + dot3(wuot[...], inner)
        r = dot3(wrt[...], upd)
        sr = sig(r)
        valid = lax.broadcasted_iota(jnp.int32, (CH, L), 1) + l < cnt
        dr = jnp.where(valid, tiled(wecol[...], L) * (sr + r * sr * (1.0 - sr)), 0.0)
        du = dot3(wr[...], dr)
        di = dot3(wuo[...], du)
        dp = di * (s + inner * (1.0 - s))
        summed[:, l:l+L] = dot3(wui[...], dp)

def stage_d(k, nbr, onehot, pt, od, dsum, own, sc):
    row = nbr[pl.ds(k, 1), :]
    hi = row >> 8
    dd = jnp.sum(dsum[...] * pt[k], axis=0, keepdims=True)
    D = od[k] * dd
    own[...] -= D
    Dh = D.astype(bf).astype(f32)
    Dl = D - Dh
    D8 = Dh + pltpu.roll(Dl, 3, axis=0)
    Gm = jnp.concatenate([jnp.where(hi == h, D8, 0.0) for h in range(8)], axis=0).astype(bf)
    sc[...] += lax.dot_general(Gm, onehot[k], (((1,), (1,)), ((), ())), preferred_element_type=f32)


class Place:
    def __init__(self):
        self.image = lax.axis_index("image")
        self.dom = lax.axis_index("dom")
        self.x = self.dom % X
        self.z = (self.dom // X) % Z
        self.y = self.dom // (X * Z)
        self.slot1 = self.y * X + self.x
        self.up = (self.image, (self.dom + 1) % DOM)
        self.down = (self.image, (self.dom + DOM - 1) % DOM)
        self.partner = (1 - self.image, self.dom)

    def peer1(self, o):
        s = (self.slot1 + o) % G1
        return (self.image, (s // X) * (X * Z) + self.z * X + s % X)

    def peer2(self, o):
        return (self.image, self.y * (X * Z) + ((self.z + o) % Z) * X + self.x)


def greet(pos, extra):
    barrier = pltpu.get_barrier_semaphore()
    peers = [pos.peer1(o) for o in range(1, G1)] + [pos.peer2(o) for o in range(1, G2)] + extra
    for peer in peers:
        pl.semaphore_signal(barrier, inc=1, device_id=peer, device_id_type=MESH)
    return barrier, len(peers)


def spread(src, dst, slot, count, peer_of, ssem, rsem):
    copies = []
    for o in range(1, count):
        copy = pltpu.make_async_remote_copy(
            src_ref=src.at[0], dst_ref=dst.at[slot], send_sem=ssem.at[o], recv_sem=rsem.at[slot],
            device_id=peer_of(o), device_id_type=MESH)
        copy.start()
        copies.append(copy)
    return copies


def gather_wait(dst, slot, count, rsem, src, ssem, peer_of):
    for o in range(1, count):
        other = (slot + o) % count
        pltpu.make_async_remote_copy(
            src_ref=src.at[0], dst_ref=dst.at[other], send_sem=ssem.at[o], recv_sem=rsem.at[other],
            device_id=peer_of(o), device_id_type=MESH).wait_recv()


def shift_of(side):
    return jnp.where(lax.broadcasted_iota(jnp.int32, (8, H), 0) == 0, side, 0.0)


def select_blocks(hi, G, blocks, first, L):
    acc = jnp.zeros((64, L), f32)
    for h in range(blocks):
        acc = jnp.where(hi == first + h, G[h * 64:h * 64 + 64], acc)
    return acc


def one_hot(lo, L):
    return jnp.where(lax.broadcasted_iota(jnp.int32, (LO, L), 0) == lo, 1.0, 0.0).astype(bf)


def twice(O):
    return jnp.concatenate([O, O], axis=0)


def pick_rows(table, idx, groups):
    lo = jnp.broadcast_to(idx & 127, (8, 128))
    hi = jnp.broadcast_to(idx >> 7, (8, 128))
    acc = jnp.zeros((8, 128), f32)
    for h in range(groups):
        v = jnp.take_along_axis(table[:, h * 128:h * 128 + 128], lo, axis=1)
        acc = jnp.where(hi == h, v, acc)
    return acc


def set_tab(tab, first, h, proj):
    hi, lo = split(proj)
    tab[(first + h) * 64:(first + h + 1) * 64, 0:LO] = hi
    tab[(first + h) * 64:(first + h + 1) * 64, LO:2 * LO] = lo


def stage_own(k, nbr, tab, onehot, pt, L=256):
    row = nbr[pl.ds(k, 1), :]
    for l in range(0, A, L):
        idx = row[:, l:l + L]
        O = one_hot(idx & (LO - 1), L)
        onehot[k, :, l:l + L] = O
        G = jnp.dot(tab[0:256, :], twice(O), preferred_element_type=f32)
        pt[k, :, l:l + L] = select_blocks(idx >> 8, G, 4, 0, L)


def stage_pair(k, nbr, tab, onehot, pos8, w1, w2, bcol, pt, summed, od, L=256):
    row = nbr[pl.ds(k, 1), :]
    g = 0.25 * ((RBF - 1) / 2.5) ** 2
    cen = lax.broadcasted_iota(jnp.int32, (RBF, L), 0).astype(f32) * 2.5 / (RBF - 1)
    bl = tiled(bcol[...], L)
    for l in range(0, A, L):
        idx = row[:, l:l + L]
        O = onehot[k, :, l:l + L]
        G = jnp.dot(tab[256:512, :], twice(O), preferred_element_type=f32)
        gt = pt[k, :, l:l + L] + select_blocks(idx >> 8, G, 4, 4, L)
        there = jnp.concatenate([pick_rows(pos8, idx[:, m:m + 128], 16) for m in range(0, L, 128)], axis=1)
        off = there - pos8[:, l:l + L]
        d = jnp.sqrt(jnp.sum(off * off, axis=0, keepdims=True) + 0.01)
        od[k, :, l:l + L] = off / d
        t = d - cen
        basis = jnp.exp(-g * (t * t))
        bp = basis * ((-2.0 * g) * t)
        pq = dot3(w1[...], jnp.concatenate([basis, bp], axis=1))
        pre = pq[:, :L] + bl
        s = sig(pre)
        hdn = pre * s
        z = (s + hdn * (1.0 - s)) * pq[:, L:]
        ff = dot3(w2[...], jnp.concatenate([hdn, z], axis=1))
        summed[:, l:l + L] += ff[:, :L] * gt
        pt[k, :, l:l + L] = ff[:, L:] * gt


def total(v):
    return jnp.sum(jnp.sum(v, axis=1, keepdims=True), axis=0, keepdims=True)


def ratio(p, m):
    return jnp.where(m > 0.0, p / jnp.where(m > 0.0, m, 1.0), 0.0)


def row_of(p, m, r):
    lane = lax.broadcasted_iota(jnp.int32, (1, 128), 1)
    return jnp.where(lane == 0, p, jnp.where(lane == 1, m, r))


def merge(ref, n):
    rows = [ref[i] for i in range(n)]
    ps, ms, rs = [[v[:, j:j + 1] for v in rows] for j in range(3)]
    p, m, r = sum(ps[1:], ps[0]), sum(ms[1:], ms[0]), sum(rs[1:], rs[0])
    return p, m, r, [ratio(a, b) for a, b in zip(ps, ms)], ms


def main_kernel(pos_ref, mode_ref, feat, nbr, cnt_ref, send_ref, wfi, bf_, wfo, wp_ref, wui_, bu, wuo_, wr_, we,
                res, tab, pm, rim, left, right, pos8, onehot, pickhot, pt, summed, od, own, sc, back, extra,
                mine, theirs, unit, w1, w2, bcol, bucol, wecol, wui, wuit, wuo, wuot, wr, wrt,
                a1s, a1, a2s, a2, b1s, b1, b2s, b2,
                hs, hr, gs, gr, xs, xr, sa1, ra1, sa2, ra2, sb1, rb1, sb2, rb2):
    pos = Place()
    barrier, count = greet(pos, [pos.up, pos.down, pos.partner])
    cnt = cnt_ref[0]
    valid = lax.broadcasted_iota(jnp.int32, (3, A), 1) < cnt
    masked = jnp.where(valid, mode_ref[...], 0.0)
    part = jnp.broadcast_to(total(masked * masked), (1, 128))
    a1s[0] = part
    a1[pl.ds(pos.slot1, 1)] = part[None]
    pm[...] = jnp.concatenate([pos_ref[...], masked, jnp.zeros((2, A), f32)], axis=0)
    wpt = wcat(wp_ref[...].T)
    for h in range(4):
        set_tab(tab, 0, h, dot3(wpt, feat[:, h * LO:(h + 1) * LO]))
    for side in range(2):
        row = send_ref[side:side + 1, :]
        for l in range(0, H, 256):
            idx = row[:, l:l + 256]
            O = one_hot(idx & (LO - 1), 256)
            pickhot[:, side * H + l:side * H + l + 256] = O
            G = jnp.dot(tab[0:256, :], twice(O), preferred_element_type=f32)
            rim[side, 0:64, l:l + 256] = select_blocks(idx >> 8, G, 4, 0, 256)
        for l in range(0, H, 128):
            rim[side, 64:72, l:l + 128] = pick_rows(pm, row[:, l:l + 128], 8)
    pl.semaphore_wait(barrier, count)
    sent = spread(a1s, a1, pos.slot1, G1, pos.peer1, sa1, ra1)
    low = pltpu.make_async_remote_copy(
        src_ref=rim.at[0], dst_ref=right, send_sem=hs.at[0], recv_sem=hr.at[0],
        device_id=pos.down, device_id_type=MESH)
    high = pltpu.make_async_remote_copy(
        src_ref=rim.at[1], dst_ref=left, send_sem=hs.at[1], recv_sem=hr.at[1],
        device_id=pos.up, device_id_type=MESH)
    low.start()
    high.start()
    sent += [low, high]

    w1[...] = wcat(wfi[...].T)
    w2[...] = wcat(wfo[...].T)
    wui[...] = wcat(wui_[...])
    wuit[...] = wcat(wui_[...].T)
    wuo[...] = wcat(wuo_[...])
    wuot[...] = wcat(wuo_[...].T)
    wr[...] = wcat(wr_[...])
    wrt[...] = wcat(wr_[...].T)
    bcol[...] = column(bf_)
    bucol[...] = column(bu)
    wecol[...] = column(we)
    summed[...] = jnp.zeros_like(summed)
    own[...] = jnp.zeros_like(own)
    sc[...] = jnp.zeros_like(sc)

    def own_slot(k, c):
        stage_own(k, nbr, tab, onehot, pt)
        return c

    lax.fori_loop(0, NBR // 2, own_slot, 0)
    gather_wait(a1, pos.slot1, G1, ra1, a1s, sa1, pos.peer1)
    part = a1[0]
    for i in range(1, G1):
        part = part + a1[i]
    a2s[0] = part
    a2[pl.ds(pos.z, 1)] = part[None]
    sent += spread(a2s, a2, pos.z, G2, pos.peer2, sa2, ra2)
    lax.fori_loop(NBR // 2, NBR, own_slot, 0)
    low.wait_recv()
    high.wait_recv()
    for h in range(2):
        set_tab(tab, 4, h, left[0:64, h * LO:(h + 1) * LO])
        set_tab(tab, 6, h, right[0:64, h * LO:(h + 1) * LO])
    gather_wait(a2, pos.z, G2, ra2, a2s, sa2, pos.peer2)
    part = a2[0]
    for i in range(1, G2):
        part = part + a2[i]
    scale = jnp.sqrt(TOTAL / part[:, 0:1])
    moves = (1.0 - 2.0 * pos.image.astype(f32)) * STEP
    zero5 = jnp.zeros((5, A), f32)
    u = pm[3:6, :] * scale
    unit[...] = jnp.concatenate([u, zero5], axis=0)
    pos8[:, 0:A] = jnp.concatenate([pm[0:3, :] + moves * u, zero5], axis=0)
    for buf, at, side in ((left, A, -1.0), (right, A + H, 1.0)):
        p = buf[64:67, :] + moves * (buf[67:70, :] * scale)
        pos8[:, at:at + H] = jnp.concatenate([p, jnp.zeros((5, H), f32)], axis=0) + shift_of(side)

    def pair_slot(k, c):
        stage_pair(k, nbr, tab, onehot, pos8, w1, w2, bcol, pt, summed, od)
        return c

    lax.fori_loop(0, NBR, pair_slot, 0)
    stage_c(summed, feat, cnt, wui, wuit, wuo, wuot, wr, wrt, bucol, wecol)

    def back_slot(k, c):
        stage_d(k, nbr, onehot, pt, od, summed, own, sc)
        return c

    lax.fori_loop(0, NBR, back_slot, 0)

    for h in range(8):
        v = sc[h * 8:h * 8 + 8, :]
        v = v + pltpu.roll(v, 5, axis=0)
        if h < 4:
            own[:, h * LO:(h + 1) * LO] += v
        else:
            back[(h - 4) // 2, :, (h % 2) * LO:(h % 2 + 1) * LO] = v
    up = pltpu.make_async_remote_copy(
        src_ref=back.at[1], dst_ref=extra.at[0], send_sem=gs.at[0], recv_sem=gr.at[0],
        device_id=pos.up, device_id_type=MESH)
    down = pltpu.make_async_remote_copy(
        src_ref=back.at[0], dst_ref=extra.at[1], send_sem=gs.at[1], recv_sem=gr.at[1],
        device_id=pos.down, device_id_type=MESH)
    up.start()
    down.start()
    row = jnp.concatenate([send_ref[0:1, :], send_ref[1:2, :]], axis=1)
    up.wait_recv()
    down.wait_recv()
    keep = lax.broadcasted_iota(jnp.int32, (8, A), 0) < 3
    D = jnp.where(keep, jnp.concatenate([extra[0], extra[1]], axis=1), 0.0)
    Dh = D.astype(bf).astype(f32)
    D8 = Dh + pltpu.roll(D - Dh, 3, axis=0)
    Gm = jnp.concatenate([jnp.where((row >> 8) == h, D8, 0.0) for h in range(4)], axis=0).astype(bf)
    S = lax.dot_general(Gm, pickhot[...], (((1,), (1,)), ((), ())), preferred_element_type=f32)
    for h in range(4):
        v = S[h * 8:h * 8 + 8, :]
        v = v + pltpu.roll(v, 5, axis=0) + own[:, h * LO:(h + 1) * LO]
        mine[:, h * LO:(h + 1) * LO] = jnp.where(keep[:, 0:LO], -v, 0.0)
    swap = pltpu.make_async_remote_copy(
        src_ref=mine, dst_ref=theirs, send_sem=xs.at[0], recv_sem=xr.at[0],
        device_id=pos.partner, device_id_type=MESH)
    swap.start()
    u = unit[...]
    res[0:8, :] = mine[...]
    res[8:16, :] = u
    m = total(u * u)
    swap.wait_recv()
    sign = 1.0 - 2.0 * pos.image.astype(f32)
    diff = sign * (mine[...] - theirs[...]) / (2.0 * STEP)
    res[16:24, :] = diff

    p = total(diff * u)
    rest = diff - ratio(p, m) * u
    packed = row_of(p, m, total(rest * rest))
    b1s[0] = packed
    b1[pl.ds(pos.slot1, 1)] = packed[None]
    sent += [up, down, swap] + spread(b1s, b1, pos.slot1, G1, pos.peer1, sb1, rb1)
    gather_wait(b1, pos.slot1, G1, rb1, b1s, sb1, pos.peer1)
    p, m, r, qs, ms = merge(b1, G1)
    q = ratio(p, m)
    for a, b in zip(qs, ms):
        r = r + (a - q) * (a - q) * b
    packed = row_of(p, m, r)
    b2s[0] = packed
    b2[pl.ds(pos.z, 1)] = packed[None]
    sent += spread(b2s, b2, pos.z, G2, pos.peer2, sb2, rb2)
    gather_wait(b2, pos.z, G2, rb2, b2s, sb2, pos.peer2)
    p, m, r, qs, ms = merge(b2, G2)
    slope = p / TOTAL
    norm = (TURN * TURN) * r
    for a, b in zip(qs, ms):
        f = 1.0 + TURN * (a - slope)
        norm = norm + f * f * b
    res[24:32, :] = jnp.broadcast_to(slope, (8, A))
    res[32:40, :] = jnp.broadcast_to(jnp.sqrt(TOTAL / norm), (8, A))
    for copy in sent:
        copy.wait_send()


def finish_kernel(res, forces, rot_out, mode_out, curv):
    first = lax.axis_index("image") == 0
    slope = res[24:25, 0:128]
    curv[...] = -slope
    u, diff = res[8:16, :], res[16:24, :]
    rot = diff - res[24:25, :] * u
    moved = (u + TURN * rot) * res[32:33, :]
    for i in range(3):
        forces[i] = res[i:i + 1, :]
        rot_out[i] = jnp.where(first, rot[i:i + 1, 0:H], rot[i:i + 1, H:A])
        mode_out[i] = jnp.where(first, moved[i:i + 1, 0:H], moved[i:i + 1, H:A])


def local(positions, mode, features, neighbours, counts, send_index, w_filter_in, b_filter, w_filter_out,
          w_project, w_update_in, b_update, w_update_out, w_readout, w_energy):
    vm = pl.BlockSpec(memory_space=pltpu.VMEM)
    sm = pl.BlockSpec(memory_space=pltpu.SMEM)
    S = jax.ShapeDtypeStruct

    def V(*s, dt=f32):
        return pltpu.VMEM(s, dt)

    dma = pltpu.SemaphoreType.DMA
    reds = [V(1, 1, 128), V(G1, 1, 128), V(1, 1, 128), V(G2, 1, 128)]
    sems = [dma((G1,)), dma((G1,)), dma((G2,)), dma((G2,))]
    res = pl.pallas_call(
        main_kernel, out_shape=S((40, A), f32),
        in_specs=[vm, vm, vm, vm, sm] + [vm] * 10, out_specs=vm,
        scratch_shapes=[
            V(512, 512, dt=bf), V(8, A), V(2, 72, H), V(72, H), V(72, H), V(8, 2 * A),
            V(NBR, LO, A, dt=bf), V(LO, A, dt=bf), V(NBR, CH, A), V(CH, A), V(NBR, 8, A), V(8, A), V(64, LO),
            V(2, 8, H), V(2, 8, H), V(8, A), V(8, A), V(8, A),
            V(64, 96, dt=bf), V(64, 192, dt=bf), V(64, 128), V(64, 128), V(64, 128)] + [V(64, 192, dt=bf)] * 6
        + reds + reds + [dma((2,))] * 4 + [dma((1,))] * 2 + sems + sems,
        compiler_params=pltpu.CompilerParams(collective_id=0, has_side_effects=True),
    )(positions, mode, features, neighbours, counts, send_index, w_filter_in, b_filter[None], w_filter_out, w_project,
      w_update_in, b_update[None], w_update_out, w_readout, w_energy[None])
    forces, rot, new_mode, curv = pl.pallas_call(
        finish_kernel, out_shape=(S((3, 1, A), f32), S((3, 1, H), f32), S((3, 1, H), f32), S((1, 128), f32)),
        in_specs=[vm], out_specs=(vm, vm, vm, vm),
    )(res)
    return (forces.transpose(1, 0, 2), rot, new_mode, curv[0, 0:1])


def solution(mesh):
    col = P(None, "dom")
    in_specs = (col, col, col, col, P("dom"), col) + (P(),) * 9
    out_specs = (P("image", None, "dom"), P(None, "image", "dom"), P(None, "image", "dom"), P())
    return jax.shard_map(local, mesh=mesh, in_specs=in_specs, out_specs=out_specs, check_vma=False)
```

```python
import functools

import jax
import jax.numpy as jnp
from jax import lax
from jax.experimental import pallas as pl
from jax.experimental.pallas import tpu as pltpu
from jax.sharding import PartitionSpec as P

f32 = jnp.float32
bf = jnp.bfloat16
CH = 64
RBF = 32
NBR = 12
A = 1024
H = 512
LO = 256
STEP = 0.05
TURN = 0.5
X, Y, Z = 4, 4, 8
G1, G2 = X * Y, Z
DOM = X * Y * Z
TOTAL = 3.0 * DOM * A
MESH = pl.DeviceIdType.MESH


def split(x):
    hi = x.astype(bf)
    return hi, (x - hi.astype(f32)).astype(bf)

def wcat(w):
    hi, lo = split(w)
    return jnp.concatenate([hi, lo, hi], axis=1)

def dot3(wc, x):
    hi, lo = split(x)
    return jnp.dot(wc, jnp.concatenate([hi, hi, lo], axis=0), preferred_element_type=f32)

def column(row_ref):
    return jnp.broadcast_to(row_ref[...], (128, row_ref.shape[1])).T

def tiled(col, L):
    return jnp.concatenate([col] * (L // 128), axis=1)

def sig(x):
    return 0.5 * jnp.tanh(0.5 * x) + 0.5

def stage_c(summed, feat, cnt, wui, wuit, wuo, wuot, wr, wrt, bucol, wecol, L=1024):
    for l in range(0, A, L):
        pre = dot3(wuit[...], summed[:, l:l+L]) + tiled(bucol[...], L)
        s = sig(pre)
        inner = pre * s
        upd = feat[:, l:l+L] + dot3(wuot[...], inner)
        r = dot3(wrt[...], upd)
        sr = sig(r)
        valid = lax.broadcasted_iota(jnp.int32, (CH, L), 1) + l < cnt
        dr = jnp.where(valid, tiled(wecol[...], L) * (sr + r * sr * (1.0 - sr)), 0.0)
        du = dot3(wr[...], dr)
        di = dot3(wuo[...], du)
        dp = di * (s + inner * (1.0 - s))
        summed[:, l:l+L] = dot3(wui[...], dp)

def back_slope(k, slopes, od, dsum, own):
    dd = jnp.sum(dsum[...] * slopes[k], axis=0, keepdims=True)
    D = od[k] * dd
    own[...] -= D
    Dh = D.astype(bf).astype(f32)
    return Dh + pltpu.roll(D - Dh, 3, axis=0)


def back_scatter(k, nbr, onehot, D8):
    hib = jnp.broadcast_to(nbr[pl.ds(k, 1), :] >> 7, (8, A))
    Gm = jnp.concatenate([jnp.where(hib == h, D8, 0.0) for h in range(16)], axis=0).astype(bf)
    O = onehot[k, 0:128, :] + onehot[k, 128:256, :]
    return lax.dot_general(Gm, O, (((1,), (1,)), ((), ())), preferred_element_type=f32)


class Place:
    def __init__(self):
        self.image = lax.axis_index("image")
        self.dom = lax.axis_index("dom")
        self.x = self.dom % X
        self.z = (self.dom // X) % Z
        self.y = self.dom // (X * Z)
        self.slot1 = self.y * X + self.x
        self.up = (self.image, (self.dom + 1) % DOM)
        self.down = (self.image, (self.dom + DOM - 1) % DOM)
        self.up2 = (1 - self.image, self.up[1])
        self.down2 = (1 - self.image, self.down[1])
        self.partner = (1 - self.image, self.dom)

    def peer1(self, o):
        s = (self.slot1 + o) % G1
        return (self.image, (s // X) * (X * Z) + self.z * X + s % X)

    def peer2(self, o):
        return (self.image, self.y * (X * Z) + ((self.z + o) % Z) * X + self.x)


def greet(pos, extra):
    barrier = pltpu.get_barrier_semaphore()
    peers = [pos.peer1(o) for o in range(1, G1)] + [pos.peer2(o) for o in range(1, G2)] + extra
    for peer in peers:
        pl.semaphore_signal(barrier, inc=1, device_id=peer, device_id_type=MESH)
    return barrier, len(peers)


def spread(src, dst, slot, count, peer_of, ssem, rsem):
    copies = []
    for o in range(1, count):
        copy = pltpu.make_async_remote_copy(
            src_ref=src.at[0], dst_ref=dst.at[slot], send_sem=ssem.at[o], recv_sem=rsem.at[slot],
            device_id=peer_of(o), device_id_type=MESH)
        copy.start()
        copies.append(copy)
    return copies


def gather_wait(dst, slot, count, rsem, src, ssem, peer_of):
    for o in range(1, count):
        other = (slot + o) % count
        pltpu.make_async_remote_copy(
            src_ref=src.at[0], dst_ref=dst.at[other], send_sem=ssem.at[o], recv_sem=rsem.at[other],
            device_id=peer_of(o), device_id_type=MESH).wait_recv()


def shift_of(side):
    return jnp.where(lax.broadcasted_iota(jnp.int32, (8, H), 0) == 0, side, 0.0)


LANE_ROWS = 24
MM = CH - LANE_ROWS


def select_blocks(hi, G, blocks, first, L, acc=None):
    hib = jnp.broadcast_to(hi, (MM, L))
    for h in range(blocks):
        block = G[h * MM:h * MM + MM]
        acc = jnp.where(hib == first + h, block, jnp.zeros((MM, L), f32) if acc is None else acc)
    return acc


def one_hot(lo, L):
    rows = lax.broadcasted_iota(jnp.int32, (LO, L), 0).astype(f32).astype(bf)
    at = jnp.broadcast_to(lo.astype(f32), (LO, L)).astype(bf)
    return jnp.where(rows == at, jnp.ones((), bf), jnp.zeros((), bf))


def pick_rows(table, idx, groups, first=0, acc=None, at=0, rows=8):
    lo = jnp.broadcast_to(idx & 127, (8, 128))
    hi = jnp.broadcast_to(idx >> 7, (8, 128))
    out = []
    for r in range(0, rows, 8):
        v = jnp.zeros((8, 128), f32) if acc is None else acc[r:r + 8]
        for h in range(groups):
            c = at + h * 128
            got = jnp.take_along_axis(table[r:r + 8, c:c + 128], lo, axis=1)
            v = jnp.where(hi == first + h, got, v)
        out.append(v)
    return jnp.concatenate(out, axis=0) if len(out) > 1 else out[0]


def set_tab(tab, h, proj):
    at = (h // 4) * (8 * MM) + (h % 4) * MM
    hi, lo = split(proj)
    tab[at:at + MM, :] = hi
    tab[at + 4 * MM:at + 5 * MM, :] = lo


def look_up(table, O):
    G = jnp.dot(table, O, preferred_element_type=f32)
    return G[0:4 * MM] + G[4 * MM:8 * MM]


def stage_own(k, nbr, tab, lanes, onehot, pt, L=256):
    row = nbr[pl.ds(k, 1), :]
    for l in range(0, A, L):
        idx = row[:, l:l + L]
        O = one_hot(idx & (LO - 1), L)
        onehot[k, :, l:l + L] = O
        pt[k, LANE_ROWS:CH, l:l + L] = select_blocks(idx >> 8, look_up(tab[0:8 * MM, :], O), 4, 0, L)
        for m in range(l, l + L, 128):
            if LANE_ROWS:
                pt[k, 0:LANE_ROWS, m:m + 128] = pick_rows(lanes, row[:, m:m + 128], 8, rows=LANE_ROWS)


def stage_rim(k, nbr, tab, lanes, onehot, pt, gt, L=256):
    row = nbr[pl.ds(k, 1), :]
    for l in range(0, A, L):
        idx = row[:, l:l + L]
        O = onehot[k, :, l:l + L]
        gt[k, LANE_ROWS:CH, l:l + L] = select_blocks(
            idx >> 8, look_up(tab[8 * MM:16 * MM, :], O), 4, 4, L, pt[k, LANE_ROWS:CH, l:l + L])
        for m in range(l, l + L, 128):
            if LANE_ROWS:
                gt[k, 0:LANE_ROWS, m:m + 128] = pick_rows(
                    lanes, row[:, m:m + 128], 8, 8, pt[k, 0:LANE_ROWS, m:m + 128], A, LANE_ROWS)


def pair_distance(k, nbr, pos8, od, dist, L=256):
    row = nbr[pl.ds(k, 1), :]
    for l in range(0, A, L):
        there = jnp.concatenate([pick_rows(pos8, row[:, m:m + 128], 16) for m in range(l, l + L, 128)], axis=1)
        off = there - pos8[:, l:l + L]
        d = jnp.sqrt(jnp.sum(off * off, axis=0, keepdims=True) + 0.01)
        od[k, :, l:l + L] = off / d
        dist[:, l:l + L] = jnp.broadcast_to(d, (8, L))


def pair_filter(w1, bcol, dist, hz, L=256):
    g = 0.25 * ((RBF - 1) / 2.5) ** 2
    bl = tiled(bcol[...], L)
    for l in range(0, A, L):
        d8 = dist[:, l:l + L]
        t = jnp.concatenate([d8] * (RBF // 8), axis=0) - (
            lax.broadcasted_iota(jnp.int32, (RBF, L), 0).astype(f32) * 2.5 / (RBF - 1))
        basis = jnp.exp(-g * (t * t))
        pq = dot3(w1[...], jnp.concatenate([basis, basis * ((-2.0 * g) * t)], axis=1))
        pre = pq[:, :L] + bl
        s = sig(pre)
        hdn = pre * s
        z = (s + hdn * (1.0 - s)) * pq[:, L:]
        for at, v in ((l, hdn), (A + l, z)):
            hi, lo = split(v)
            hz[0:64, at:at + L] = hi
            hz[64:128, at:at + L] = lo


def pair_apply(k, w2, hz, gt, slopes, summed, L=256):
    for l in range(0, A, L):
        both = []
        for at in (l, A + l):
            hi, lo = hz[0:64, at:at + L], hz[64:128, at:at + L]
            both.append(jnp.dot(w2[...], jnp.concatenate([hi, hi, lo], axis=0), preferred_element_type=f32))
        g = gt[k, :, l:l + L]
        summed[:, l:l + L] += both[0] * g
        slopes[k, :, l:l + L] = both[1] * g


def total(v):
    return jnp.sum(jnp.sum(v, axis=1, keepdims=True), axis=0, keepdims=True)


def ratio(p, m):
    return jnp.where(m > 0.0, p / jnp.where(m > 0.0, m, 1.0), 0.0)


def row_of(p, m, r):
    lane = lax.broadcasted_iota(jnp.int32, (1, 128), 1)
    return jnp.where(lane == 0, p, jnp.where(lane == 1, m, r))


def merge(ref, n):
    rows = [ref[i] for i in range(n)]
    ps, ms, rs = [[v[:, j:j + 1] for v in rows] for j in range(3)]
    p, m, r = sum(ps[1:], ps[0]), sum(ms[1:], ms[0]), sum(rs[1:], rs[0])
    return p, m, r, [ratio(a, b) for a, b in zip(ps, ms)], ms


SCR_NAMES = (
    "tab", "lanes", "pm", "rim", "left", "right", "pos8", "onehot", "pickhot", "pt", "gt", "slopes", "hz", "dist",
    "summed", "od", "own", "sc", "back", "extra", "mine", "theirs", "unit",
    "w1", "w2", "bcol", "bucol", "wecol", "wui", "wuit", "wuo", "wuot", "wr", "wrt")


def scratch():
    def V(*s, dt=f32):
        return pltpu.VMEM(s, dt)

    return [
        V(16 * MM, LO, dt=bf), V(max(LANE_ROWS, 8), 2 * A), V(8, A), V(2, 72, H), V(72, H), V(72, H), V(8, 2 * A),
        V(NBR, LO, A, dt=bf), V(128, A, dt=bf), V(NBR, CH, A), V(NBR, CH, A), V(NBR, CH, A),
        V(2 * CH, 2 * A, dt=bf), V(8, A), V(CH, A), V(NBR, 8, A), V(8, A), V(128, 128),
        V(2, 8, H), V(2, 2, 8, H), V(8, A), V(8, A), V(8, A),
        V(64, 96, dt=bf), V(64, 192, dt=bf), V(64, 128), V(64, 128), V(64, 128)] + [V(64, 192, dt=bf)] * 6


def prep(sd, wfi, bf_, wfo, wui_, bu, wuo_, wr_, we):
    sd["w1"][...] = wcat(wfi[...].T)
    sd["w2"][...] = wcat(wfo[...].T)
    for name, ref in (("wui", wui_), ("wuo", wuo_), ("wr", wr_)):
        sd[name][...] = wcat(ref[...])
        sd[name + "t"][...] = wcat(ref[...].T)
    sd["bcol"][...] = column(bf_)
    sd["bucol"][...] = column(bu)
    sd["wecol"][...] = column(we)
    for name in ("summed", "own", "sc"):
        sd[name][...] = jnp.zeros_like(sd[name])


def run_own(sd, nbr, first, last):
    def body(k, c):
        stage_own(k, nbr, sd["tab"], sd["lanes"], sd["onehot"], sd["pt"])
        return c

    lax.fori_loop(first, last, body, 0)


def run_rim(sd, nbr):
    def body(k, c):
        stage_rim(k, nbr, sd["tab"], sd["lanes"], sd["onehot"], sd["pt"], sd["gt"])
        return c

    lax.fori_loop(0, NBR, body, 0)


def run_pair(sd, nbr):
    def distance(k):
        pair_distance(k, nbr, sd["pos8"], sd["od"], sd["dist"])

    def hidden():
        pair_filter(sd["w1"], sd["bcol"], sd["dist"], sd["hz"])

    def apply(k):
        pair_apply(k, sd["w2"], sd["hz"], sd["gt"], sd["slopes"], sd["summed"])

    def body(k, c):
        apply(k - 2)
        hidden()
        distance(k)
        return c

    distance(0)
    hidden()
    distance(1)
    lax.fori_loop(2, NBR, body, 0)
    apply(NBR - 2)
    hidden()
    apply(NBR - 1)


def run_update(sd, feat, cnt):
    stage_c(sd["summed"], feat, cnt, sd["wui"], sd["wuit"], sd["wuo"], sd["wuot"], sd["wr"], sd["wrt"],
            sd["bucol"], sd["wecol"])


BACK_UNROLL = 6


def run_back(sd, nbr):
    def body(i, c):
        acc = sd["sc"][...]
        for j in range(BACK_UNROLL):
            k = i * BACK_UNROLL + j
            D8 = back_slope(k, sd["slopes"], sd["od"], sd["summed"], sd["own"])
            acc = acc + back_scatter(k, nbr, sd["onehot"], D8)
        sd["sc"][...] = acc
        return c

    lax.fori_loop(0, NBR // BACK_UNROLL, body, 0)


def grad_block(sd, h):
    v = jnp.concatenate([sd["sc"][16 * h:16 * h + 8, :], sd["sc"][16 * h + 8:16 * h + 16, :]], axis=1)
    v = v + pltpu.roll(v, 5, axis=0)
    return v + sd["own"][:, h * LO:(h + 1) * LO] if h < 4 else v


def push(src, dst, send_sem, recv_sem, peer):
    copy = pltpu.make_async_remote_copy(
        src_ref=src, dst_ref=dst, send_sem=send_sem, recv_sem=recv_sem, device_id=peer, device_id_type=MESH)
    copy.start()
    return copy


def main_kernel(pos_ref, mode_ref, feat, nbr, cnt_ref, send_ref, wfi, bf_, wfo, wp_ref, wui_, bu, wuo_, wr_, we,
                res, *scr):
    sd = dict(zip(SCR_NAMES, scr))
    tab, lanes, pm, rim, left, right, pos8 = [sd[n] for n in ("tab", "lanes", "pm", "rim", "left", "right", "pos8")]
    pickhot, own, back, extra = [sd[n] for n in ("pickhot", "own", "back", "extra")]
    mine, theirs, unit = [sd[n] for n in ("mine", "theirs", "unit")]
    (a1s, a1, a2s, a2, b1s, b1, b2s, b2, hs, hr, gs, gr, xs, xr,
     sa1, ra1, sa2, ra2, sb1, rb1, sb2, rb2) = scr[len(SCR_NAMES):]
    pos = Place()
    barrier, count = greet(pos, [pos.up, pos.down, pos.partner, pos.up2, pos.down2])
    cnt = cnt_ref[0]
    valid = lax.broadcasted_iota(jnp.int32, (3, A), 1) < cnt
    masked = jnp.where(valid, mode_ref[...], 0.0)
    part = jnp.broadcast_to(total(masked * masked), (1, 128))
    a1s[0] = part
    a1[pl.ds(pos.slot1, 1)] = part[None]
    pm[...] = jnp.concatenate([pos_ref[...], masked, jnp.zeros((2, A), f32)], axis=0)
    wpt = wcat(wp_ref[...].T)
    for h in range(4):
        proj = dot3(wpt, feat[:, h * LO:(h + 1) * LO])
        lanes[:, h * LO:(h + 1) * LO] = proj[0:LANE_ROWS]
        set_tab(tab, h, proj[LANE_ROWS:])
    for side in range(2):
        row = send_ref[side:side + 1, :]
        for l in range(0, H, 256):
            idx = row[:, l:l + 256]
            O = one_hot(idx & (LO - 1), 256)
            pickhot[:, side * H + l:side * H + l + 256] = O[0:128] + O[128:256]
            rim[side, LANE_ROWS:CH, l:l + 256] = select_blocks(idx >> 8, look_up(tab[0:8 * MM, :], O), 4, 0, 256)
        for l in range(0, H, 128):
            rim[side, 0:LANE_ROWS, l:l + 128] = pick_rows(lanes, row[:, l:l + 128], 8, rows=LANE_ROWS)
            rim[side, CH:CH + 8, l:l + 128] = pick_rows(pm, row[:, l:l + 128], 8)
    pl.semaphore_wait(barrier, count)
    sent = spread(a1s, a1, pos.slot1, G1, pos.peer1, sa1, ra1)
    low = push(rim.at[0], right, hs.at[0], hr.at[0], pos.down)
    high = push(rim.at[1], left, hs.at[1], hr.at[1], pos.up)
    sent += [low, high]

    prep(sd, wfi, bf_, wfo, wui_, bu, wuo_, wr_, we)
    run_own(sd, nbr, 0, NBR)
    gather_wait(a1, pos.slot1, G1, ra1, a1s, sa1, pos.peer1)
    part = a1[0]
    for i in range(1, G1):
        part = part + a1[i]
    a2s[0] = part
    a2[pl.ds(pos.z, 1)] = part[None]
    sent += spread(a2s, a2, pos.z, G2, pos.peer2, sa2, ra2)
    low.wait_recv()
    high.wait_recv()
    for buf, at in ((left, 4), (right, 6)):
        lanes[:, at * LO:(at + 2) * LO] = buf[0:LANE_ROWS, :]
        for h in range(2):
            set_tab(tab, at + h, buf[LANE_ROWS:CH, h * LO:(h + 1) * LO])
    run_rim(sd, nbr)
    gather_wait(a2, pos.z, G2, ra2, a2s, sa2, pos.peer2)
    part = a2[0]
    for i in range(1, G2):
        part = part + a2[i]
    scale = jnp.sqrt(TOTAL / part[:, 0:1])
    sign = 1.0 - 2.0 * pos.image.astype(f32)
    moves = sign * STEP
    zero5 = jnp.zeros((5, A), f32)
    u = pm[3:6, :] * scale
    unit[...] = jnp.concatenate([u, zero5], axis=0)
    pos8[:, 0:A] = jnp.concatenate([pm[0:3, :] + moves * u, zero5], axis=0)
    for buf, at, side in ((left, A, -1.0), (right, A + H, 1.0)):
        p = buf[CH:CH + 3, :] + moves * (buf[CH + 3:CH + 6, :] * scale)
        pos8[:, at:at + H] = jnp.concatenate([p, jnp.zeros((5, H), f32)], axis=0) + shift_of(side)

    run_pair(sd, nbr)
    run_update(sd, feat, cnt)
    run_back(sd, nbr)

    keep = lax.broadcasted_iota(jnp.int32, (8, A), 0) < 3
    for h in range(4, 8):
        back[(h - 4) // 2, :, (h % 2) * LO:(h % 2 + 1) * LO] = grad_block(sd, h)
    for h in range(4):
        mine[:, h * LO:(h + 1) * LO] = jnp.where(keep[:, 0:LO], grad_block(sd, h), 0.0)
    moved = [push(back.at[1], extra.at[0, 0], gs.at[0], gr.at[0], pos.up),
             push(back.at[0], extra.at[0, 1], gs.at[1], gr.at[1], pos.down),
             push(back.at[1], extra.at[1, 0], gs.at[2], gr.at[2], pos.up2),
             push(back.at[0], extra.at[1, 1], gs.at[3], gr.at[3], pos.down2),
             push(mine, theirs, xs.at[0], xr.at[0], pos.partner)]
    sent += moved
    u = unit[...]
    m = total(u * u)
    row = jnp.concatenate([send_ref[0:1, :], send_ref[1:2, :]], axis=1)
    hib = jnp.broadcast_to(row >> 7, (8, A))
    masks = [hib == h for h in range(8)]
    for copy in moved:
        copy.wait_recv()
    halves = []
    for i in range(2):
        D = jnp.where(keep, jnp.concatenate([extra[i, 0], extra[i, 1]], axis=1), 0.0)
        Dh = D.astype(bf).astype(f32)
        D8 = Dh + pltpu.roll(D - Dh, 3, axis=0)
        halves += [jnp.where(mask, D8, 0.0) for mask in masks]
    Gm = jnp.concatenate(halves, axis=0).astype(bf)
    S = lax.dot_general(Gm, pickhot[...], (((1,), (1,)), ((), ())), preferred_element_type=f32)
    force = []
    for i, ref in ((0, mine), (1, theirs)):
        v = jnp.concatenate([S[64 * i + 8 * h:64 * i + 8 * h + 8, :] for h in range(8)], axis=1)
        v = v + pltpu.roll(v, 5, axis=0)
        force.append(jnp.where(keep, -(ref[...] + v), 0.0))
    res[0:8, :] = force[0]
    diff = (sign / (2.0 * STEP)) * (force[0] - force[1])

    p = total(diff * u)
    rest = diff - ratio(p, m) * u
    packed = row_of(p, m, total(rest * rest))
    b1s[0] = packed
    b1[pl.ds(pos.slot1, 1)] = packed[None]
    sent += spread(b1s, b1, pos.slot1, G1, pos.peer1, sb1, rb1)
    gather_wait(b1, pos.slot1, G1, rb1, b1s, sb1, pos.peer1)
    p, m, r, qs, ms = merge(b1, G1)
    q = ratio(p, m)
    for a, b in zip(qs, ms):
        r = r + (a - q) * (a - q) * b
    packed = row_of(p, m, r)
    b2s[0] = packed
    b2[pl.ds(pos.z, 1)] = packed[None]
    sent += spread(b2s, b2, pos.z, G2, pos.peer2, sb2, rb2)
    gather_wait(b2, pos.z, G2, rb2, b2s, sb2, pos.peer2)
    p, m, r, qs, ms = merge(b2, G2)
    slope = p / TOTAL
    norm = (TURN * TURN) * r
    for a, b in zip(qs, ms):
        f = 1.0 + TURN * (a - slope)
        norm = norm + f * f * b
    first = pos.image == 0
    uh = jnp.where(first, u[:, 0:H], u[:, H:A])
    rot = jnp.where(first, diff[:, 0:H], diff[:, H:A]) - slope * uh
    new = (uh + TURN * rot) * jnp.sqrt(TOTAL / norm)
    res[8:16, :] = jnp.where(keep, jnp.concatenate([rot, new], axis=1), -slope)
    for copy in sent:
        copy.wait_send()


def finish_kernel(res, forces, rot_out, mode_out, curv):
    curv[...] = res[11:12, 0:128]
    for i in range(3):
        forces[i] = res[i:i + 1, :]
        rot_out[i] = res[8 + i:9 + i, 0:H]
        mode_out[i] = res[8 + i:9 + i, H:A]


def local(positions, mode, features, neighbours, counts, send_index, w_filter_in, b_filter, w_filter_out,
          w_project, w_update_in, b_update, w_update_out, w_readout, w_energy):
    vm = pl.BlockSpec(memory_space=pltpu.VMEM)
    sm = pl.BlockSpec(memory_space=pltpu.SMEM)
    S = jax.ShapeDtypeStruct

    def V(*s, dt=f32):
        return pltpu.VMEM(s, dt)

    dma = pltpu.SemaphoreType.DMA
    reds = [V(1, 1, 128), V(G1, 1, 128), V(1, 1, 128), V(G2, 1, 128)]
    sems = [dma((G1,)), dma((G1,)), dma((G2,)), dma((G2,))]
    res = pl.pallas_call(
        main_kernel, out_shape=S((16, A), f32),
        in_specs=[vm, vm, vm, vm, sm] + [vm] * 10, out_specs=vm,
        scratch_shapes=scratch()
        + reds + reds + [dma((2,))] * 2 + [dma((4,))] * 2 + [dma((1,))] * 2 + sems + sems,
        compiler_params=pltpu.CompilerParams(collective_id=0, has_side_effects=True),
    )(positions, mode, features, neighbours, counts, send_index, w_filter_in, b_filter[None], w_filter_out, w_project,
      w_update_in, b_update[None], w_update_out, w_readout, w_energy[None])
    forces, rot, new_mode, curv = pl.pallas_call(
        finish_kernel, out_shape=(S((3, 1, A), f32), S((3, 1, H), f32), S((3, 1, H), f32), S((1, 128), f32)),
        in_specs=[vm], out_specs=(vm, vm, vm, vm),
    )(res)
    return (forces.transpose(1, 0, 2), rot, new_mode, curv[0, 0:1])


def solution(mesh):
    col = P(None, "dom")
    in_specs = (col, col, col, col, P("dom"), col) + (P(),) * 9
    out_specs = (P("image", None, "dom"), P(None, "image", "dom"), P(None, "image", "dom"), P())
    return jax.shard_map(local, mesh=mesh, in_specs=in_specs, out_specs=out_specs, check_vma=False)
```

```python
import functools

import jax
import jax.numpy as jnp
from jax import lax
from jax.experimental import pallas as pl
from jax.experimental.pallas import tpu as pltpu
from jax.sharding import PartitionSpec as P

f32 = jnp.float32
bf = jnp.bfloat16
CH = 64
RBF = 32
NBR = 12
A = 1024
H = 512
LO = 256
STEP = 0.05
TURN = 0.5
X, Y, Z = 4, 4, 8
G1, G2 = X * Y, Z
DOM = X * Y * Z
TOTAL = 3.0 * DOM * A
MESH = pl.DeviceIdType.MESH


def split(x):
    hi = x.astype(bf)
    return hi, (x - hi.astype(f32)).astype(bf)

def wcat(w):
    hi, lo = split(w)
    return jnp.concatenate([hi, lo, hi], axis=1)

def dot3(wc, x):
    hi, lo = split(x)
    return jnp.dot(wc, jnp.concatenate([hi, hi, lo], axis=0), preferred_element_type=f32)

def column(row_ref):
    return jnp.broadcast_to(row_ref[...], (128, row_ref.shape[1])).T

def tiled(col, L):
    return jnp.concatenate([col] * (L // 128), axis=1)

def sig(x):
    return 0.5 * jnp.tanh(0.5 * x) + 0.5

def stage_c(summed, feat, cnt, wui, wuit, wuo, wuot, wr, wrt, bucol, wecol, L=1024):
    for l in range(0, A, L):
        pre = dot3(wuit[...], summed[:, l:l+L]) + tiled(bucol[...], L)
        s = sig(pre)
        inner = pre * s
        upd = feat[:, l:l+L] + dot3(wuot[...], inner)
        r = dot3(wrt[...], upd)
        sr = sig(r)
        valid = lax.broadcasted_iota(jnp.int32, (CH, L), 1) + l < cnt
        dr = jnp.where(valid, tiled(wecol[...], L) * (sr + r * sr * (1.0 - sr)), 0.0)
        du = dot3(wr[...], dr)
        di = dot3(wuo[...], du)
        dp = di * (s + inner * (1.0 - s))
        summed[:, l:l+L] = dot3(wui[...], dp)

def back_slope(k, slopes, od, dsum, own):
    dd = jnp.sum(dsum[...] * slopes[k], axis=0, keepdims=True)
    D = od[k] * dd
    own[...] -= D
    Dh = D.astype(bf).astype(f32)
    return Dh + pltpu.roll(D - Dh, 3, axis=0)


def back_scatter(k, nbr, onehot, D8, first):
    hib = jnp.broadcast_to(nbr[pl.ds(k, 1), :] >> 7, (8, A))
    Gm = jnp.concatenate([jnp.where(hib == first + h, D8, 0.0) for h in range(8)], axis=0).astype(bf)
    O = onehot[k, 0:128, :] + onehot[k, 128:256, :]
    return lax.dot_general(Gm, O, (((1,), (1,)), ((), ())), preferred_element_type=f32)


class Place:
    def __init__(self):
        self.image = lax.axis_index("image")
        self.dom = lax.axis_index("dom")
        self.x = self.dom % X
        self.z = (self.dom // X) % Z
        self.y = self.dom // (X * Z)
        self.slot1 = self.y * X + self.x
        self.up = (self.image, (self.dom + 1) % DOM)
        self.down = (self.image, (self.dom + DOM - 1) % DOM)
        self.up2 = (1 - self.image, self.up[1])
        self.down2 = (1 - self.image, self.down[1])
        self.partner = (1 - self.image, self.dom)

    def peer1(self, o):
        y, x = (self.y + o // X) % Y, (self.x + o % X) % X
        return (self.image, y * (X * Z) + self.z * X + x), y * X + x

    def peer2(self, o):
        z = (self.z + o) % Z
        return (self.image, self.y * (X * Z) + z * X + self.x), z


def hops(o, n):
    return min(o, n - o)


ORDER1 = sorted(range(1, G1), key=lambda o: -hops(o // X, Y) - hops(o % X, X))
ORDER2 = sorted(range(1, G2), key=lambda o: -hops(o, Z))


def greet(pos, extra):
    barrier = pltpu.get_barrier_semaphore()
    peers = [pos.peer2(o)[0] for o in ORDER2] + [pos.peer1(o)[0] for o in ORDER1] + extra
    for peer in peers:
        pl.semaphore_signal(barrier, inc=1, device_id=peer, device_id_type=MESH)
    return barrier, len(peers)


def spread(src, dst, slot, order, peer_of, ssem, rsem):
    copies = []
    for o in order:
        copy = pltpu.make_async_remote_copy(
            src_ref=src.at[0], dst_ref=dst.at[slot], send_sem=ssem.at[o], recv_sem=rsem.at[slot],
            device_id=peer_of(o)[0], device_id_type=MESH)
        copy.start()
        copies.append(copy)
    return copies


def gather_wait(dst, order, rsem, src, ssem, peer_of):
    for o in reversed(order):
        device, other = peer_of(o)
        pltpu.make_async_remote_copy(
            src_ref=src.at[0], dst_ref=dst.at[other], send_sem=ssem.at[o], recv_sem=rsem.at[other],
            device_id=device, device_id_type=MESH).wait_recv()


LANE_ROWS = 24
MM = CH - LANE_ROWS


def select_blocks(hi, G, blocks, first, L, acc=None):
    hib = jnp.broadcast_to(hi, (MM, L))
    for h in range(blocks):
        block = G[h * MM:h * MM + MM]
        acc = jnp.where(hib == first + h, block, jnp.zeros((MM, L), f32) if acc is None else acc)
    return acc


def one_hot(lo, L):
    rows = lax.broadcasted_iota(jnp.int32, (LO, L), 0).astype(f32).astype(bf)
    at = jnp.broadcast_to(lo.astype(f32), (LO, L)).astype(bf)
    return jnp.where(rows == at, jnp.ones((), bf), jnp.zeros((), bf))


def pick_rows(table, idx, groups, first=0, acc=None, at=0, rows=8):
    lo = jnp.broadcast_to(idx & 127, (8, 128))
    hi = jnp.broadcast_to(idx >> 7, (8, 128))
    out = []
    for r in range(0, rows, 8):
        v = jnp.zeros((8, 128), f32) if acc is None else acc[r:r + 8]
        for h in range(groups):
            c = at + h * 128
            got = jnp.take_along_axis(table[r:r + 8, c:c + 128], lo, axis=1)
            v = jnp.where(hi == first + h, got, v)
        out.append(v)
    return jnp.concatenate(out, axis=0) if len(out) > 1 else out[0]


def set_tab(tab, h, proj):
    at = (h // 4) * (8 * MM) + (h % 4) * MM
    hi, lo = split(proj)
    tab[at:at + MM, :] = hi
    tab[at + 4 * MM:at + 5 * MM, :] = lo


def look_up(table, O):
    G = jnp.dot(table, O, preferred_element_type=f32)
    return G[0:4 * MM] + G[4 * MM:8 * MM]


def stage_own(k, nbr, tab, lanes, onehot, pt, L=256):
    row = nbr[pl.ds(k, 1), :]
    for l in range(0, A, L):
        idx = row[:, l:l + L]
        O = one_hot(idx & (LO - 1), L)
        onehot[k, :, l:l + L] = O
        pt[k, LANE_ROWS:CH, l:l + L] = select_blocks(idx >> 8, look_up(tab[0:8 * MM, :], O), 4, 0, L)
        for m in range(l, l + L, 128):
            if LANE_ROWS:
                pt[k, 0:LANE_ROWS, m:m + 128] = pick_rows(lanes, row[:, m:m + 128], 8, rows=LANE_ROWS)


def stage_rim(k, nbr, tab, lanes, onehot, pt, gt, L=256):
    row = nbr[pl.ds(k, 1), :]
    for l in range(0, A, L):
        idx = row[:, l:l + L]
        O = onehot[k, :, l:l + L]
        gt[k, LANE_ROWS:CH, l:l + L] = select_blocks(
            idx >> 8, look_up(tab[8 * MM:16 * MM, :], O), 4, 4, L, pt[k, LANE_ROWS:CH, l:l + L])
        for m in range(l, l + L, 128):
            if LANE_ROWS:
                gt[k, 0:LANE_ROWS, m:m + 128] = pick_rows(
                    lanes, row[:, m:m + 128], 8, 8, pt[k, 0:LANE_ROWS, m:m + 128], A, LANE_ROWS)


SHARP = 0.25 * ((RBF - 1) / 2.5) ** 2
KAPPA = (SHARP * 1.4426950408889634) ** 0.5


def pick_position(pos8, idx):
    wide = jnp.broadcast_to(idx, (8, 128))
    lo = wide & 127
    bit = [(wide & (128 << i)) != 0 for i in range(4)]
    v = [jnp.take_along_axis(pos8[:, h * 128:h * 128 + 128], lo, axis=1) for h in range(8)]
    for i in range(3):
        v = [jnp.where(bit[i], v[j + 1], v[j]) for j in range(0, len(v), 2)]
    return jnp.where(bit[3], pltpu.roll(v[0], 4, axis=0), v[0])


def pair_distance(k, nbr, pos8, od, dist, L=256):
    row = nbr[pl.ds(k, 1), :]
    keep = lax.broadcasted_iota(jnp.int32, (8, L), 0) < 3
    for l in range(0, A, L):
        there = jnp.concatenate([pick_position(pos8, row[:, m:m + 128]) for m in range(l, l + L, 128)], axis=1)
        off = jnp.where(keep, there - pos8[:, l:l + L], 0.0)
        d = jnp.sqrt(jnp.sum(off * off, axis=0, keepdims=True) + 0.01)
        od[k, :, l:l + L] = off * ((-2.0 * SHARP / KAPPA) / d)
        dist[:, l:l + L] = jnp.broadcast_to(KAPPA * d, (8, L))


def pair_filter(w1, dist, hz, L=256):
    one = jnp.where(
        (lax.broadcasted_iota(jnp.int32, (16, 2 * L), 0) < 3) & (lax.broadcasted_iota(jnp.int32, (16, 2 * L), 1) < L),
        1.0, 0.0).astype(bf)
    cen = lax.broadcasted_iota(jnp.int32, (RBF, L), 0).astype(f32) * (KAPPA * 2.5 / (RBF - 1))
    for l in range(0, A, L):
        t = jnp.concatenate([dist[:, l:l + L]] * (RBF // 8), axis=0) - cen
        basis = jnp.exp2(-(t * t))
        hi, lo = split(jnp.concatenate([basis, basis * t], axis=1))
        pq = jnp.dot(w1[...], jnp.concatenate([hi, hi, lo, one], axis=0), preferred_element_type=f32)
        a = pq[:, :L]
        th = jnp.tanh(a)
        p = 1.0 + th
        hdn = a * p
        z = (p * (1.0 + a * (1.0 - th))) * pq[:, L:]
        for at, v in ((l, hdn), (A + l, z)):
            hi, lo = split(v)
            hz[0:64, at:at + L] = hi
            hz[64:128, at:at + L] = lo


def pair_apply(k, w2, hz, gt, slopes, summed, L=256):
    for l in range(0, A, L):
        both = []
        for at in (l, A + l):
            hi, lo = hz[0:64, at:at + L], hz[64:128, at:at + L]
            both.append(jnp.dot(w2[...], jnp.concatenate([hi, hi, lo], axis=0), preferred_element_type=f32))
        g = gt[k, :, l:l + L]
        summed[:, l:l + L] += both[0] * g
        slopes[k, :, l:l + L] = both[1] * g


def total(v):
    return jnp.sum(jnp.sum(v, axis=1, keepdims=True), axis=0, keepdims=True)


def ratio(p, m):
    return jnp.where(m > 0.0, p / jnp.where(m > 0.0, m, 1.0), 0.0)


def row_of(p, m, r):
    lane = lax.broadcasted_iota(jnp.int32, (1, 128), 1)
    return jnp.where(lane == 0, p, jnp.where(lane == 1, m, r))


def merge(ref):
    rows = ref[:, 0, :]
    p, m, r = rows[:, 0:1], rows[:, 1:2], rows[:, 2:3]
    sums = [jnp.sum(v, axis=0, keepdims=True) for v in (p, m, r)]
    return sums, ratio(p, m), m


SCR_NAMES = (
    "tab", "lanes", "pm", "rim", "left", "right", "pos8", "onehot", "pickhot", "pt", "gt", "slopes", "hz", "dist",
    "summed", "od", "d8", "own", "sc", "back", "extra", "mine", "theirs", "unit",
    "w1", "w2", "bucol", "wecol", "wui", "wuit", "wuo", "wuot", "wr", "wrt")


def scratch():
    def V(*s, dt=f32):
        return pltpu.VMEM(s, dt)

    return [
        V(16 * MM, LO, dt=bf), V(max(LANE_ROWS, 8), 2 * A), V(8, A), V(2, 72, H), V(72, H), V(72, H), V(8, A),
        V(NBR, LO, A, dt=bf), V(128, A, dt=bf), V(NBR, CH, A), V(NBR, CH, A), V(NBR, CH, A),
        V(2 * CH, 2 * A, dt=bf), V(8, A), V(CH, A), V(NBR, 8, A), V(NBR, 8, A), V(8, A), V(128, 128),
        V(2, 8, H), V(2, 2, 8, H), V(8, A), V(8, A), V(8, A),
        V(64, 112, dt=bf), V(64, 192, dt=bf), V(64, 128), V(64, 128)] + [V(64, 192, dt=bf)] * 6


def prep(sd, wfi, bf_, wfo, wui_, bu, wuo_, wr_, we):
    sd["w1"][:, 0:96] = wcat(0.5 * wfi[...].T)
    bias = 0.5 * column(bf_)[:, 0:16]
    b_hi = bias.astype(bf)
    b_mid, b_lo = split(bias - b_hi.astype(f32))
    lane = lax.broadcasted_iota(jnp.int32, (64, 16), 1)
    aug = jnp.where(lane == 0, b_hi.astype(f32), jnp.where(lane == 1, b_mid.astype(f32), b_lo.astype(f32)))
    sd["w1"][:, 96:112] = jnp.where(lane < 3, aug, 0.0).astype(bf)
    sd["w2"][...] = wcat(wfo[...].T)
    for name, ref in (("wui", wui_), ("wuo", wuo_), ("wr", wr_)):
        sd[name][...] = wcat(ref[...])
        sd[name + "t"][...] = wcat(ref[...].T)
    sd["bucol"][...] = column(bu)
    sd["wecol"][...] = column(we)
    for name in ("summed", "own", "sc"):
        sd[name][...] = jnp.zeros_like(sd[name])


LOOK_UNROLL = 6


def run_own(sd, nbr):
    def body(i, c):
        for j in range(LOOK_UNROLL):
            stage_own(i * LOOK_UNROLL + j, nbr, sd["tab"], sd["lanes"], sd["onehot"], sd["pt"])
        return c

    lax.fori_loop(0, NBR // LOOK_UNROLL, body, 0)


def run_rim(sd, nbr):
    def body(i, c):
        for j in range(LOOK_UNROLL):
            stage_rim(i * LOOK_UNROLL + j, nbr, sd["tab"], sd["lanes"], sd["onehot"], sd["pt"], sd["gt"])
        return c

    lax.fori_loop(0, NBR // LOOK_UNROLL, body, 0)


def run_pair(sd, nbr):
    def distance(k):
        pair_distance(k, nbr, sd["pos8"], sd["od"], sd["dist"])

    def hidden():
        pair_filter(sd["w1"], sd["dist"], sd["hz"])

    def apply(k):
        pair_apply(k, sd["w2"], sd["hz"], sd["gt"], sd["slopes"], sd["summed"])

    def body(k, c):
        apply(k - 2)
        hidden()
        distance(k)
        return c

    distance(0)
    hidden()
    distance(1)
    lax.fori_loop(2, NBR, body, 0)
    apply(NBR - 2)
    hidden()
    apply(NBR - 1)


def run_update(sd, feat, cnt):
    stage_c(sd["summed"], feat, cnt, sd["wui"], sd["wuit"], sd["wuo"], sd["wuot"], sd["wr"], sd["wrt"],
            sd["bucol"], sd["wecol"])


BACK_UNROLL = 6


def run_back(sd, nbr, part):
    def body(i, c):
        acc = sd["sc"][64 * part:64 * part + 64, :]
        for j in range(BACK_UNROLL):
            k = i * BACK_UNROLL + j
            if part:
                D8 = back_slope(k, sd["slopes"], sd["od"], sd["summed"], sd["own"])
                sd["d8"][k] = D8
            else:
                D8 = sd["d8"][k]
            acc = acc + back_scatter(k, nbr, sd["onehot"], D8, 8 * part)
        sd["sc"][64 * part:64 * part + 64, :] = acc
        return c

    lax.fori_loop(0, NBR // BACK_UNROLL, body, 0)


def grad_block(sd, h):
    v = jnp.concatenate([sd["sc"][16 * h:16 * h + 8, :], sd["sc"][16 * h + 8:16 * h + 16, :]], axis=1)
    v = v + pltpu.roll(v, 5, axis=0)
    return v + sd["own"][:, h * LO:(h + 1) * LO] if h < 4 else v


def push(src, dst, send_sem, recv_sem, peer):
    copy = pltpu.make_async_remote_copy(
        src_ref=src, dst_ref=dst, send_sem=send_sem, recv_sem=recv_sem, device_id=peer, device_id_type=MESH)
    copy.start()
    return copy


LOAD_ORDER = (1, 4, 0, 9, 2, 5, 3, 6, 7, 8, 10, 11, 12, 13, 14)


def main_kernel(*refs):
    inputs, res, held, load_sem, scr = refs[:15], refs[15], refs[16:31], refs[31], refs[32:]
    loads = [pltpu.make_async_copy(inputs[i], held[i], load_sem.at[i]) for i in range(15)]
    for i in LOAD_ORDER:
        loads[i].start()
    pos_ref, mode_ref, feat, nbr, cnt_ref, send_ref, wfi, bf_, wfo, wp_ref, wui_, bu, wuo_, wr_, we = held
    sd = dict(zip(SCR_NAMES, scr))
    tab, lanes, pm, rim, left, right, pos8 = [sd[n] for n in ("tab", "lanes", "pm", "rim", "left", "right", "pos8")]
    pickhot, own, back, extra = [sd[n] for n in ("pickhot", "own", "back", "extra")]
    mine, theirs, unit = [sd[n] for n in ("mine", "theirs", "unit")]
    (a1s, a1, a2s, a2, b1s, b1, b2s, b2, hs, hr, gs, gr, xs, xr,
     sa1, ra1, sa2, ra2, sb1, rb1, sb2, rb2) = scr[len(SCR_NAMES):]
    pos = Place()
    barrier, count = greet(pos, [pos.up, pos.down, pos.partner, pos.up2, pos.down2])
    for i in LOAD_ORDER[:3]:
        loads[i].wait()
    cnt = jnp.broadcast_to(cnt_ref[...], (8, 128))
    valid = lax.broadcasted_iota(jnp.int32, (3, A), 1) < cnt[0:1, 0:1]
    masked = jnp.where(valid, mode_ref[...], 0.0)
    part = jnp.broadcast_to(total(masked * masked), (1, 128))
    a1s[0] = part
    a1[pl.ds(pos.slot1, 1)] = part[None]
    pm[...] = jnp.concatenate([pos_ref[...], masked, jnp.zeros((2, A), f32)], axis=0)
    for i in LOAD_ORDER[3:6]:
        loads[i].wait()
    wpt = wcat(wp_ref[...].T)
    for h in range(4):
        proj = dot3(wpt, feat[:, h * LO:(h + 1) * LO])
        lanes[:, h * LO:(h + 1) * LO] = proj[0:LANE_ROWS]
        set_tab(tab, h, proj[LANE_ROWS:])
    for side in range(2):
        row = send_ref[side:side + 1, :]
        for l in range(0, H, 256):
            idx = row[:, l:l + 256]
            O = one_hot(idx & (LO - 1), 256)
            pickhot[:, side * H + l:side * H + l + 256] = O[0:128] + O[128:256]
            rim[side, LANE_ROWS:CH, l:l + 256] = select_blocks(idx >> 8, look_up(tab[0:8 * MM, :], O), 4, 0, 256)
        for l in range(0, H, 128):
            rim[side, 0:LANE_ROWS, l:l + 128] = pick_rows(lanes, row[:, l:l + 128], 8, rows=LANE_ROWS)
            rim[side, CH:CH + 8, l:l + 128] = pick_rows(pm, row[:, l:l + 128], 8)
    for i in LOAD_ORDER[6:]:
        loads[i].wait()
    prep(sd, wfi, bf_, wfo, wui_, bu, wuo_, wr_, we)
    pl.semaphore_wait(barrier, count)
    low = push(rim.at[0], right, hs.at[0], hr.at[0], pos.down)
    high = push(rim.at[1], left, hs.at[1], hr.at[1], pos.up)
    sent = [low, high] + spread(a1s, a1, pos.slot1, ORDER1, pos.peer1, sa1, ra1)

    run_own(sd, nbr)
    gather_wait(a1, ORDER1, ra1, a1s, sa1, pos.peer1)
    part = jnp.sum(a1[:, 0, :], axis=0, keepdims=True)
    a2s[0] = part
    a2[pl.ds(pos.z, 1)] = part[None]
    sent += spread(a2s, a2, pos.z, ORDER2, pos.peer2, sa2, ra2)
    low.wait_recv()
    high.wait_recv()
    for buf, at in ((left, 4), (right, 6)):
        lanes[:, at * LO:(at + 2) * LO] = buf[0:LANE_ROWS, :]
        for h in range(2):
            set_tab(tab, at + h, buf[LANE_ROWS:CH, h * LO:(h + 1) * LO])
    run_rim(sd, nbr)
    gather_wait(a2, ORDER2, ra2, a2s, sa2, pos.peer2)
    part = jnp.sum(a2[:, 0, :], axis=0, keepdims=True)
    scale = jnp.sqrt(TOTAL / part[:, 0:1])
    sign = 1.0 - 2.0 * pos.image.astype(f32)
    moves = sign * STEP
    u = pm[3:6, :] * scale
    unit[...] = jnp.concatenate([u, jnp.zeros((5, A), f32)], axis=0)
    shift = jnp.where(lax.broadcasted_iota(jnp.int32, (3, H), 0) == 0, 1.0, 0.0)
    sides = [buf[CH:CH + 3, :] + moves * (buf[CH + 3:CH + 6, :] * scale) for buf in (left, right)]
    beside = jnp.concatenate([sides[0] - shift, sides[1] + shift], axis=1)
    gap = jnp.zeros((1, A), f32)
    pos8[...] = jnp.concatenate([pm[0:3, :] + moves * u, gap, beside, gap], axis=0)

    run_pair(sd, nbr)
    run_update(sd, feat, cnt[0:1, 0:1])
    run_back(sd, nbr, 1)

    keep = lax.broadcasted_iota(jnp.int32, (8, A), 0) < 3
    for h in range(4, 8):
        back[(h - 4) // 2, :, (h % 2) * LO:(h % 2 + 1) * LO] = grad_block(sd, h)
    moved = [push(back.at[1], extra.at[0, 0], gs.at[0], gr.at[0], pos.up),
             push(back.at[0], extra.at[0, 1], gs.at[1], gr.at[1], pos.down),
             push(back.at[1], extra.at[1, 0], gs.at[2], gr.at[2], pos.up2),
             push(back.at[0], extra.at[1, 1], gs.at[3], gr.at[3], pos.down2)]
    run_back(sd, nbr, 0)
    for h in range(4):
        mine[:, h * LO:(h + 1) * LO] = jnp.where(keep[:, 0:LO], grad_block(sd, h), 0.0)
    moved += [push(mine, theirs, xs.at[0], xr.at[0], pos.partner)]
    for copy in sent:
        copy.wait_send()
    sent = moved
    u = unit[...]
    m = total(u * u)
    row = jnp.concatenate([send_ref[0:1, :], send_ref[1:2, :]], axis=1)
    hib = jnp.broadcast_to(row >> 7, (8, A))
    masks = [hib == h for h in range(8)]
    for copy in moved:
        copy.wait_recv()
    halves = []
    for i in range(2):
        D = jnp.where(keep, jnp.concatenate([extra[i, 0], extra[i, 1]], axis=1), 0.0)
        Dh = D.astype(bf).astype(f32)
        D8 = Dh + pltpu.roll(D - Dh, 3, axis=0)
        halves += [jnp.where(mask, D8, 0.0) for mask in masks]
    Gm = jnp.concatenate(halves, axis=0).astype(bf)
    S = lax.dot_general(Gm, pickhot[...], (((1,), (1,)), ((), ())), preferred_element_type=f32)
    force = []
    for i, ref in ((0, mine), (1, theirs)):
        v = jnp.concatenate([S[64 * i + 8 * h:64 * i + 8 * h + 8, :] for h in range(8)], axis=1)
        v = v + pltpu.roll(v, 5, axis=0)
        force.append(jnp.where(keep, -(ref[...] + v), 0.0))
    res[0:8, :] = force[0]
    diff = (sign / (2.0 * STEP)) * (force[0] - force[1])

    p = total(diff * u)
    rest = diff - ratio(p, m) * u
    packed = row_of(p, m, total(rest * rest))
    b1s[0] = packed
    b1[pl.ds(pos.slot1, 1)] = packed[None]
    sent += spread(b1s, b1, pos.slot1, ORDER1, pos.peer1, sb1, rb1)
    gather_wait(b1, ORDER1, rb1, b1s, sb1, pos.peer1)
    (p, m, r), qs, ms = merge(b1)
    away = qs - ratio(p, m)
    packed = row_of(p, m, r + jnp.sum(away * away * ms, axis=0, keepdims=True))
    b2s[0] = packed
    b2[pl.ds(pos.z, 1)] = packed[None]
    last = spread(b2s, b2, pos.z, ORDER2, pos.peer2, sb2, rb2)
    for copy in sent:
        copy.wait_send()
    gather_wait(b2, ORDER2, rb2, b2s, sb2, pos.peer2)
    (p, m, r), qs, ms = merge(b2)
    slope = p / TOTAL
    along = 1.0 + TURN * (qs - slope)
    norm = (TURN * TURN) * r + jnp.sum(along * along * ms, axis=0, keepdims=True)
    first = pos.image == 0
    uh = jnp.where(first, u[:, 0:H], u[:, H:A])
    rot = jnp.where(first, diff[:, 0:H], diff[:, H:A]) - slope * uh
    new = (uh + TURN * rot) * jnp.sqrt(TOTAL / norm)
    res[8:16, :] = jnp.where(keep, jnp.concatenate([rot, new], axis=1), -slope)
    for copy in last:
        copy.wait_send()


def finish_kernel(res, forces, rot_out, mode_out, curv):
    curv[...] = res[11:12, 0:128]
    for i in range(3):
        forces[i] = res[i:i + 1, :]
        rot_out[i] = res[8 + i:9 + i, 0:H]
        mode_out[i] = res[8 + i:9 + i, H:A]


def local(positions, mode, features, neighbours, counts, send_index, w_filter_in, b_filter, w_filter_out,
          w_project, w_update_in, b_update, w_update_out, w_readout, w_energy):
    vm = pl.BlockSpec(memory_space=pltpu.VMEM)
    hbm = pl.BlockSpec(memory_space=pltpu.HBM)
    S = jax.ShapeDtypeStruct

    def V(*s, dt=f32):
        return pltpu.VMEM(s, dt)

    dma = pltpu.SemaphoreType.DMA
    reds = [V(1, 1, 128), V(G1, 1, 128), V(1, 1, 128), V(G2, 1, 128)]
    sems = [dma((G1,)), dma((G1,)), dma((G2,)), dma((G2,))]
    args = (
        positions, mode, features, neighbours, counts.reshape(1, 1), send_index, w_filter_in, b_filter[None], w_filter_out,
        w_project, w_update_in, b_update[None], w_update_out, w_readout, w_energy[None])
    res = pl.pallas_call(
        main_kernel, out_shape=S((16, A), f32),
        in_specs=[hbm] * 15, out_specs=vm,
        scratch_shapes=[pltpu.VMEM(v.shape, v.dtype) for v in args] + [dma((15,))] + scratch()
        + reds + reds + [dma((2,))] * 2 + [dma((4,))] * 2 + [dma((1,))] * 2 + sems + sems,
        compiler_params=pltpu.CompilerParams(collective_id=0, has_side_effects=True),
    )(*args)
    forces, rot, new_mode, curv = pl.pallas_call(
        finish_kernel, out_shape=(S((3, 1, A), f32), S((3, 1, H), f32), S((3, 1, H), f32), S((1, 128), f32)),
        in_specs=[vm], out_specs=(vm, vm, vm, vm), compiler_params=pltpu.CompilerParams(vmem_limit_bytes=4 << 20),
    )(res)
    return (forces.transpose(1, 0, 2), rot, new_mode, curv[0, 0:1])


def solution(mesh):
    col = P(None, "dom")
    in_specs = (col, col, col, col, P("dom"), col) + (P(),) * 9
    out_specs = (P("image", None, "dom"), P(None, "image", "dom"), P(None, "image", "dom"), P())
    return jax.shard_map(local, mesh=mesh, in_specs=in_specs, out_specs=out_specs, check_vma=False)
```

```python
import functools

import jax
import jax.numpy as jnp
from jax import lax
from jax.experimental import pallas as pl
from jax.experimental.pallas import tpu as pltpu
from jax.sharding import PartitionSpec as P

f32 = jnp.float32
bf = jnp.bfloat16
CH = 64
RBF = 32
NBR = 12
A = 1024
H = 512
LO = 256
STEP = 0.05
TURN = 0.5
X, Y, Z = 4, 4, 8
G1, G2 = X * Y, Z
DOM = X * Y * Z
TOTAL = 3.0 * DOM * A
MESH = pl.DeviceIdType.MESH


def split(x):
    hi = x.astype(bf)
    return hi, (x - hi.astype(f32)).astype(bf)

def wcat(w):
    hi, lo = split(w)
    return jnp.concatenate([hi, lo, hi], axis=1)

def dot3(wc, x):
    hi, lo = split(x)
    return jnp.dot(wc, jnp.concatenate([hi, hi, lo], axis=0), preferred_element_type=f32)

def column(row_ref):
    return jnp.broadcast_to(row_ref[...], (128, row_ref.shape[1])).T

def tiled(col, L):
    return jnp.concatenate([col] * (L // 128), axis=1)

def sig(x):
    return 0.5 * jnp.tanh(0.5 * x) + 0.5

def stage_c(summed, feat, cnt, wui, wuit, wuo, wuot, wr, wrt, bucol, wecol, L=1024):
    for l in range(0, A, L):
        pre = dot3(wuit[...], summed[:, l:l+L]) + tiled(bucol[...], L)
        s = sig(pre)
        inner = pre * s
        upd = feat[:, l:l+L] + dot3(wuot[...], inner)
        r = dot3(wrt[...], upd)
        sr = sig(r)
        valid = lax.broadcasted_iota(jnp.int32, (CH, L), 1) + l < cnt
        dr = jnp.where(valid, tiled(wecol[...], L) * (sr + r * sr * (1.0 - sr)), 0.0)
        du = dot3(wr[...], dr)
        di = dot3(wuo[...], du)
        dp = di * (s + inner * (1.0 - s))
        summed[:, l:l+L] = dot3(wui[...], dp)

def back_slope(k, slopes, od, dsum, own):
    dd = jnp.sum(dsum[...] * slopes[k], axis=0, keepdims=True)
    D = od[k] * dd
    own[...] -= D
    Dh = D.astype(bf).astype(f32)
    return Dh + pltpu.roll(D - Dh, 3, axis=0)


def back_scatter(k, nbr, onehot, D8, first):
    hib = jnp.broadcast_to(nbr[pl.ds(k, 1), :] >> 7, (8, A))
    Gm = jnp.concatenate([jnp.where(hib == first + h, D8, 0.0) for h in range(8)], axis=0).astype(bf)
    O = onehot[k, 0:128, :] + onehot[k, 128:256, :]
    return lax.dot_general(Gm, O, (((1,), (1,)), ((), ())), preferred_element_type=f32)


class Place:
    def __init__(self):
        self.image = lax.axis_index("image")
        self.dom = lax.axis_index("dom")
        self.x = self.dom % X
        self.z = (self.dom // X) % Z
        self.y = self.dom // (X * Z)
        self.slot1 = self.y * X + self.x
        self.up = (self.image, (self.dom + 1) % DOM)
        self.down = (self.image, (self.dom + DOM - 1) % DOM)
        self.up2 = (1 - self.image, self.up[1])
        self.down2 = (1 - self.image, self.down[1])
        self.partner = (1 - self.image, self.dom)

    def peer1(self, o):
        y, x = (self.y + o // X) % Y, (self.x + o % X) % X
        return (self.image, y * (X * Z) + self.z * X + x), y * X + x

    def peer2(self, o):
        z = (self.z + o) % Z
        return (self.image, self.y * (X * Z) + z * X + self.x), z


def hops(o, n):
    return min(o, n - o)


ORDER1 = sorted(range(1, G1), key=lambda o: -hops(o // X, Y) - hops(o % X, X))
ORDER2 = sorted(range(1, G2), key=lambda o: -hops(o, Z))


def greet(pos, extra):
    barrier = pltpu.get_barrier_semaphore()
    peers = [pos.peer2(o)[0] for o in ORDER2] + [pos.peer1(o)[0] for o in ORDER1] + extra
    for peer in peers:
        pl.semaphore_signal(barrier, inc=1, device_id=peer, device_id_type=MESH)
    return barrier, len(peers)


def spread(src, dst, slot, order, peer_of, ssem, rsem):
    copies = []
    for o in order:
        copy = pltpu.make_async_remote_copy(
            src_ref=src.at[0], dst_ref=dst.at[slot], send_sem=ssem.at[o], recv_sem=rsem.at[slot],
            device_id=peer_of(o)[0], device_id_type=MESH)
        copy.start()
        copies.append(copy)
    return copies


def gather_wait(dst, order, rsem, src, ssem, peer_of):
    for o in reversed(order):
        device, other = peer_of(o)
        pltpu.make_async_remote_copy(
            src_ref=src.at[0], dst_ref=dst.at[other], send_sem=ssem.at[o], recv_sem=rsem.at[other],
            device_id=device, device_id_type=MESH).wait_recv()


LANE_ROWS = 24
MM = CH - LANE_ROWS


def select_blocks(hi, G, blocks, first, L, acc=None):
    hib = jnp.broadcast_to(hi, (MM, L))
    for h in range(blocks):
        block = G[h * MM:h * MM + MM]
        acc = jnp.where(hib == first + h, block, jnp.zeros((MM, L), f32) if acc is None else acc)
    return acc


def one_hot(lo, L):
    rows = lax.broadcasted_iota(jnp.int32, (LO, L), 0).astype(f32).astype(bf)
    at = jnp.broadcast_to(lo.astype(f32), (LO, L)).astype(bf)
    return jnp.where(rows == at, jnp.ones((), bf), jnp.zeros((), bf))


def pick_rows(table, idx, groups, first=0, acc=None, at=0, rows=8):
    lo = jnp.broadcast_to(idx & 127, (8, 128))
    hi = jnp.broadcast_to(idx >> 7, (8, 128))
    out = []
    for r in range(0, rows, 8):
        v = jnp.zeros((8, 128), f32) if acc is None else acc[r:r + 8]
        for h in range(groups):
            c = at + h * 128
            got = jnp.take_along_axis(table[r:r + 8, c:c + 128], lo, axis=1)
            v = jnp.where(hi == first + h, got, v)
        out.append(v)
    return jnp.concatenate(out, axis=0) if len(out) > 1 else out[0]


def set_tab(tab, h, proj):
    at = (h // 4) * (8 * MM) + (h % 4) * MM
    hi, lo = split(proj)
    tab[at:at + MM, :] = hi
    tab[at + 4 * MM:at + 5 * MM, :] = lo


def look_up(table, O):
    G = jnp.dot(table, O, preferred_element_type=f32)
    return G[0:4 * MM] + G[4 * MM:8 * MM]


def stage_own(k, nbr, tab, lanes, onehot, pt, L=256):
    row = nbr[pl.ds(k, 1), :]
    for l in range(0, A, L):
        idx = row[:, l:l + L]
        O = one_hot(idx & (LO - 1), L)
        onehot[k, :, l:l + L] = O
        pt[k, LANE_ROWS:CH, l:l + L] = select_blocks(idx >> 8, look_up(tab[0:8 * MM, :], O), 4, 0, L)
        for m in range(l, l + L, 128):
            if LANE_ROWS:
                pt[k, 0:LANE_ROWS, m:m + 128] = pick_rows(lanes, row[:, m:m + 128], 8, rows=LANE_ROWS)


def stage_rim(k, nbr, tab, lanes, onehot, pt, gt, L=256):
    row = nbr[pl.ds(k, 1), :]
    for l in range(0, A, L):
        idx = row[:, l:l + L]
        O = onehot[k, :, l:l + L]
        gt[k, LANE_ROWS:CH, l:l + L] = select_blocks(
            idx >> 8, look_up(tab[8 * MM:16 * MM, :], O), 4, 4, L, pt[k, LANE_ROWS:CH, l:l + L])
        for m in range(l, l + L, 128):
            if LANE_ROWS:
                gt[k, 0:LANE_ROWS, m:m + 128] = pick_rows(
                    lanes, row[:, m:m + 128], 8, 8, pt[k, 0:LANE_ROWS, m:m + 128], A, LANE_ROWS)


SHARP = 0.25 * ((RBF - 1) / 2.5) ** 2
LOG2E = 1.4426950408889634


def pick_position(pos8, idx):
    wide = jnp.broadcast_to(idx, (8, 128))
    lo = wide & 127
    bit = [(wide & (128 << i)) != 0 for i in range(4)]
    v = [jnp.take_along_axis(pos8[:, h * 128:h * 128 + 128], lo, axis=1) for h in range(8)]
    for i in range(3):
        v = [jnp.where(bit[i], v[j + 1], v[j]) for j in range(0, len(v), 2)]
    return jnp.where(bit[3], pltpu.roll(v[0], 4, axis=0), v[0])


def pair_distance(k, nbr, pos8, od, dist, L=256):
    row = nbr[pl.ds(k, 1), :]
    keep = lax.broadcasted_iota(jnp.int32, (8, L), 0) < 3
    for l in range(0, A, L):
        there = jnp.concatenate([pick_position(pos8, row[:, m:m + 128]) for m in range(l, l + L, 128)], axis=1)
        off = jnp.where(keep, there - pos8[:, l:l + L], 0.0)
        d = jnp.sqrt(jnp.sum(off * off, axis=0, keepdims=True) + 0.01)
        od[k, :, l:l + L] = off * ((-2.0 * SHARP) / d)
        dist[:, l:l + L] = jnp.broadcast_to(d, (8, L))


def pair_filter(w1, dist, hz, L=256):
    one = jnp.where(
        (lax.broadcasted_iota(jnp.int32, (16, 2 * L), 0) < 3) & (lax.broadcasted_iota(jnp.int32, (16, 2 * L), 1) < L),
        1.0, 0.0).astype(bf)
    cen = lax.broadcasted_iota(jnp.int32, (RBF, L), 0).astype(f32) * 2.5 / (RBF - 1)
    for l in range(0, A, L):
        t = jnp.concatenate([dist[:, l:l + L]] * (RBF // 8), axis=0) - cen
        basis = jnp.exp2((t * t) * (-SHARP * LOG2E))
        hi, lo = split(jnp.concatenate([basis, basis * t], axis=1))
        pq = jnp.dot(w1[...], jnp.concatenate([hi, hi, lo, one], axis=0), preferred_element_type=f32)
        a = pq[:, :L]
        th = jnp.tanh(a)
        p = 1.0 + th
        hdn = a * p
        z = (p * (1.0 + a * (1.0 - th))) * pq[:, L:]
        for at, v in ((l, hdn), (A + l, z)):
            hi, lo = split(v)
            hz[0:64, at:at + L] = hi
            hz[64:128, at:at + L] = lo


def pair_apply(k, w2, hz, gt, slopes, summed, L=256):
    for l in range(0, A, L):
        both = []
        for at in (l, A + l):
            hi, lo = hz[0:64, at:at + L], hz[64:128, at:at + L]
            both.append(jnp.dot(w2[...], jnp.concatenate([hi, hi, lo], axis=0), preferred_element_type=f32))
        g = gt[k, :, l:l + L]
        summed[:, l:l + L] += both[0] * g
        slopes[k, :, l:l + L] = both[1] * g


def total(v):
    return jnp.sum(jnp.sum(v, axis=1, keepdims=True), axis=0, keepdims=True)


def ratio(p, m):
    return jnp.where(m > 0.0, p / jnp.where(m > 0.0, m, 1.0), 0.0)


def row_of(p, m, r):
    lane = lax.broadcasted_iota(jnp.int32, (1, 128), 1)
    return jnp.where(lane == 0, p, jnp.where(lane == 1, m, r))


def merge(ref):
    rows = ref[:, 0, :]
    p, m, r = rows[:, 0:1], rows[:, 1:2], rows[:, 2:3]
    sums = [jnp.sum(v, axis=0, keepdims=True) for v in (p, m, r)]
    return sums, ratio(p, m), m


SCR_NAMES = (
    "tab", "lanes", "pm", "rim", "left", "right", "pos8", "onehot", "pickhot", "pt", "gt", "slopes", "hz", "dist",
    "summed", "od", "d8", "own", "sc", "back", "extra", "mine", "theirs", "unit",
    "w1", "w2", "bucol", "wecol", "wui", "wuit", "wuo", "wuot", "wr", "wrt")


def scratch():
    def V(*s, dt=f32):
        return pltpu.VMEM(s, dt)

    return [
        V(16 * MM, LO, dt=bf), V(max(LANE_ROWS, 8), 2 * A), V(8, A), V(2, 72, H), V(72, H), V(72, H), V(8, A),
        V(NBR, LO, A, dt=bf), V(128, A, dt=bf), V(NBR, CH, A), V(NBR, CH, A), V(NBR, CH, A),
        V(2 * CH, 2 * A, dt=bf), V(8, A), V(CH, A), V(NBR, 8, A), V(NBR, 8, A), V(8, A), V(128, 128),
        V(2, 8, H), V(2, 2, 8, H), V(8, A), V(8, A), V(8, A),
        V(64, 112, dt=bf), V(64, 192, dt=bf), V(64, 128), V(64, 128)] + [V(64, 192, dt=bf)] * 6


def prep(sd, wfi, bf_, wfo, wui_, bu, wuo_, wr_, we):
    sd["w1"][:, 0:96] = wcat(0.5 * wfi[...].T)
    bias = 0.5 * column(bf_)[:, 0:16]
    b_hi = bias.astype(bf)
    b_mid, b_lo = split(bias - b_hi.astype(f32))
    lane = lax.broadcasted_iota(jnp.int32, (64, 16), 1)
    aug = jnp.where(lane == 0, b_hi.astype(f32), jnp.where(lane == 1, b_mid.astype(f32), b_lo.astype(f32)))
    sd["w1"][:, 96:112] = jnp.where(lane < 3, aug, 0.0).astype(bf)
    sd["w2"][...] = wcat(wfo[...].T)
    for name, ref in (("wui", wui_), ("wuo", wuo_), ("wr", wr_)):
        sd[name][...] = wcat(ref[...])
        sd[name + "t"][...] = wcat(ref[...].T)
    sd["bucol"][...] = column(bu)
    sd["wecol"][...] = column(we)
    for name in ("summed", "own", "sc"):
        sd[name][...] = jnp.zeros_like(sd[name])


LOOK_UNROLL = 6


def run_own(sd, nbr):
    def body(i, c):
        for j in range(LOOK_UNROLL):
            stage_own(i * LOOK_UNROLL + j, nbr, sd["tab"], sd["lanes"], sd["onehot"], sd["pt"])
        return c

    lax.fori_loop(0, NBR // LOOK_UNROLL, body, 0)


def run_rim(sd, nbr):
    def body(i, c):
        for j in range(LOOK_UNROLL):
            stage_rim(i * LOOK_UNROLL + j, nbr, sd["tab"], sd["lanes"], sd["onehot"], sd["pt"], sd["gt"])
        return c

    lax.fori_loop(0, NBR // LOOK_UNROLL, body, 0)


def run_pair(sd, nbr):
    def distance(k):
        pair_distance(k, nbr, sd["pos8"], sd["od"], sd["dist"])

    def hidden():
        pair_filter(sd["w1"], sd["dist"], sd["hz"])

    def apply(k):
        pair_apply(k, sd["w2"], sd["hz"], sd["gt"], sd["slopes"], sd["summed"])

    def body(k, c):
        apply(k - 2)
        hidden()
        distance(k)
        return c

    distance(0)
    hidden()
    distance(1)
    lax.fori_loop(2, NBR, body, 0)
    apply(NBR - 2)
    hidden()
    apply(NBR - 1)


def run_update(sd, feat, cnt):
    stage_c(sd["summed"], feat, cnt, sd["wui"], sd["wuit"], sd["wuo"], sd["wuot"], sd["wr"], sd["wrt"],
            sd["bucol"], sd["wecol"])


BACK_UNROLL = 6


def run_back(sd, nbr, part):
    def body(i, c):
        acc = sd["sc"][64 * part:64 * part + 64, :]
        for j in range(BACK_UNROLL):
            k = i * BACK_UNROLL + j
            if part:
                D8 = back_slope(k, sd["slopes"], sd["od"], sd["summed"], sd["own"])
                sd["d8"][k] = D8
            else:
                D8 = sd["d8"][k]
            acc = acc + back_scatter(k, nbr, sd["onehot"], D8, 8 * part)
        sd["sc"][64 * part:64 * part + 64, :] = acc
        return c

    lax.fori_loop(0, NBR // BACK_UNROLL, body, 0)


def grad_block(sd, h):
    v = jnp.concatenate([sd["sc"][16 * h:16 * h + 8, :], sd["sc"][16 * h + 8:16 * h + 16, :]], axis=1)
    v = v + pltpu.roll(v, 5, axis=0)
    return v + sd["own"][:, h * LO:(h + 1) * LO] if h < 4 else v


def push(src, dst, send_sem, recv_sem, peer):
    copy = pltpu.make_async_remote_copy(
        src_ref=src, dst_ref=dst, send_sem=send_sem, recv_sem=recv_sem, device_id=peer, device_id_type=MESH)
    copy.start()
    return copy


LOAD_ORDER = (1, 4, 0, 9, 2, 5, 3, 6, 7, 8, 10, 11, 12, 13, 14)


def main_kernel(*refs):
    inputs, res, held, load_sem, scr = refs[:15], refs[15], refs[16:31], refs[31], refs[32:]
    loads = [pltpu.make_async_copy(inputs[i], held[i], load_sem.at[i]) for i in range(15)]
    for i in LOAD_ORDER:
        loads[i].start()
    pos_ref, mode_ref, feat, nbr, cnt_ref, send_ref, wfi, bf_, wfo, wp_ref, wui_, bu, wuo_, wr_, we = held
    sd = dict(zip(SCR_NAMES, scr))
    tab, lanes, pm, rim, left, right, pos8 = [sd[n] for n in ("tab", "lanes", "pm", "rim", "left", "right", "pos8")]
    pickhot, own, back, extra = [sd[n] for n in ("pickhot", "own", "back", "extra")]
    mine, theirs, unit = [sd[n] for n in ("mine", "theirs", "unit")]
    (a1s, a1, a2s, a2, b1s, b1, b2s, b2, hs, hr, gs, gr, xs, xr,
     sa1, ra1, sa2, ra2, sb1, rb1, sb2, rb2) = scr[len(SCR_NAMES):]
    pos = Place()
    barrier, count = greet(pos, [pos.up, pos.down, pos.partner, pos.up2, pos.down2])
    for i in LOAD_ORDER[:3]:
        loads[i].wait()
    cnt = jnp.broadcast_to(cnt_ref[...], (8, 128))
    valid = lax.broadcasted_iota(jnp.int32, (3, A), 1) < cnt[0:1, 0:1]
    masked = jnp.where(valid, mode_ref[...], 0.0)
    part = jnp.broadcast_to(total(masked * masked), (1, 128))
    a1s[0] = part
    a1[pl.ds(pos.slot1, 1)] = part[None]
    pm[...] = jnp.concatenate([pos_ref[...], masked, jnp.zeros((2, A), f32)], axis=0)
    for i in LOAD_ORDER[3:6]:
        loads[i].wait()
    wpt = wcat(wp_ref[...].T)
    for h in range(4):
        proj = dot3(wpt, feat[:, h * LO:(h + 1) * LO])
        lanes[:, h * LO:(h + 1) * LO] = proj[0:LANE_ROWS]
        set_tab(tab, h, proj[LANE_ROWS:])
    for side in range(2):
        row = send_ref[side:side + 1, :]
        for l in range(0, H, 256):
            idx = row[:, l:l + 256]
            O = one_hot(idx & (LO - 1), 256)
            pickhot[:, side * H + l:side * H + l + 256] = O[0:128] + O[128:256]
            rim[side, LANE_ROWS:CH, l:l + 256] = select_blocks(idx >> 8, look_up(tab[0:8 * MM, :], O), 4, 0, 256)
        for l in range(0, H, 128):
            rim[side, 0:LANE_ROWS, l:l + 128] = pick_rows(lanes, row[:, l:l + 128], 8, rows=LANE_ROWS)
            rim[side, CH:CH + 8, l:l + 128] = pick_rows(pm, row[:, l:l + 128], 8)
    for i in LOAD_ORDER[6:]:
        loads[i].wait()
    prep(sd, wfi, bf_, wfo, wui_, bu, wuo_, wr_, we)
    pl.semaphore_wait(barrier, count)
    sent = spread(a1s, a1, pos.slot1, ORDER1, pos.peer1, sa1, ra1)
    low = push(rim.at[0], right, hs.at[0], hr.at[0], pos.down)
    high = push(rim.at[1], left, hs.at[1], hr.at[1], pos.up)
    sent += [low, high]

    run_own(sd, nbr)
    gather_wait(a1, ORDER1, ra1, a1s, sa1, pos.peer1)
    part = jnp.sum(a1[:, 0, :], axis=0, keepdims=True)
    a2s[0] = part
    a2[pl.ds(pos.z, 1)] = part[None]
    sent += spread(a2s, a2, pos.z, ORDER2, pos.peer2, sa2, ra2)
    low.wait_recv()
    high.wait_recv()
    for buf, at in ((left, 4), (right, 6)):
        lanes[:, at * LO:(at + 2) * LO] = buf[0:LANE_ROWS, :]
        for h in range(2):
            set_tab(tab, at + h, buf[LANE_ROWS:CH, h * LO:(h + 1) * LO])
    run_rim(sd, nbr)
    gather_wait(a2, ORDER2, ra2, a2s, sa2, pos.peer2)
    part = jnp.sum(a2[:, 0, :], axis=0, keepdims=True)
    scale = jnp.sqrt(TOTAL / part[:, 0:1])
    sign = 1.0 - 2.0 * pos.image.astype(f32)
    moves = sign * STEP
    u = pm[3:6, :] * scale
    unit[...] = jnp.concatenate([u, jnp.zeros((5, A), f32)], axis=0)
    shift = jnp.where(lax.broadcasted_iota(jnp.int32, (3, H), 0) == 0, 1.0, 0.0)
    sides = [buf[CH:CH + 3, :] + moves * (buf[CH + 3:CH + 6, :] * scale) for buf in (left, right)]
    beside = jnp.concatenate([sides[0] - shift, sides[1] + shift], axis=1)
    gap = jnp.zeros((1, A), f32)
    pos8[...] = jnp.concatenate([pm[0:3, :] + moves * u, gap, beside, gap], axis=0)

    run_pair(sd, nbr)
    run_update(sd, feat, cnt[0:1, 0:1])
    run_back(sd, nbr, 1)

    keep = lax.broadcasted_iota(jnp.int32, (8, A), 0) < 3
    for h in range(4, 8):
        back[(h - 4) // 2, :, (h % 2) * LO:(h % 2 + 1) * LO] = grad_block(sd, h)
    moved = [push(back.at[1], extra.at[0, 0], gs.at[0], gr.at[0], pos.up),
             push(back.at[0], extra.at[0, 1], gs.at[1], gr.at[1], pos.down),
             push(back.at[1], extra.at[1, 0], gs.at[2], gr.at[2], pos.up2),
             push(back.at[0], extra.at[1, 1], gs.at[3], gr.at[3], pos.down2)]
    run_back(sd, nbr, 0)
    for h in range(4):
        mine[:, h * LO:(h + 1) * LO] = jnp.where(keep[:, 0:LO], grad_block(sd, h), 0.0)
    moved += [push(mine, theirs, xs.at[0], xr.at[0], pos.partner)]
    for copy in sent:
        copy.wait_send()
    sent = moved
    u = unit[...]
    m = total(u * u)
    row = jnp.concatenate([send_ref[0:1, :], send_ref[1:2, :]], axis=1)
    hib = jnp.broadcast_to(row >> 7, (8, A))
    masks = [hib == h for h in range(8)]
    for copy in moved:
        copy.wait_recv()
    halves = []
    for i in range(2):
        D = jnp.where(keep, jnp.concatenate([extra[i, 0], extra[i, 1]], axis=1), 0.0)
        Dh = D.astype(bf).astype(f32)
        D8 = Dh + pltpu.roll(D - Dh, 3, axis=0)
        halves += [jnp.where(mask, D8, 0.0) for mask in masks]
    Gm = jnp.concatenate(halves, axis=0).astype(bf)
    S = lax.dot_general(Gm, pickhot[...], (((1,), (1,)), ((), ())), preferred_element_type=f32)
    force = []
    for i, ref in ((0, mine), (1, theirs)):
        v = jnp.concatenate([S[64 * i + 8 * h:64 * i + 8 * h + 8, :] for h in range(8)], axis=1)
        v = v + pltpu.roll(v, 5, axis=0)
        force.append(jnp.where(keep, -(ref[...] + v), 0.0))
    res[0:8, :] = force[0]
    diff = (sign / (2.0 * STEP)) * (force[0] - force[1])

    p = total(diff * u)
    rest = diff - ratio(p, m) * u
    packed = row_of(p, m, total(rest * rest))
    b1s[0] = packed
    b1[pl.ds(pos.slot1, 1)] = packed[None]
    sent += spread(b1s, b1, pos.slot1, ORDER1, pos.peer1, sb1, rb1)
    gather_wait(b1, ORDER1, rb1, b1s, sb1, pos.peer1)
    (p, m, r), qs, ms = merge(b1)
    away = qs - ratio(p, m)
    packed = row_of(p, m, r + jnp.sum(away * away * ms, axis=0, keepdims=True))
    b2s[0] = packed
    b2[pl.ds(pos.z, 1)] = packed[None]
    last = spread(b2s, b2, pos.z, ORDER2, pos.peer2, sb2, rb2)
    for copy in sent:
        copy.wait_send()
    gather_wait(b2, ORDER2, rb2, b2s, sb2, pos.peer2)
    (p, m, r), qs, ms = merge(b2)
    slope = p / TOTAL
    along = 1.0 + TURN * (qs - slope)
    norm = (TURN * TURN) * r + jnp.sum(along * along * ms, axis=0, keepdims=True)
    first = pos.image == 0
    uh = jnp.where(first, u[:, 0:H], u[:, H:A])
    rot = jnp.where(first, diff[:, 0:H], diff[:, H:A]) - slope * uh
    new = (uh + TURN * rot) * jnp.sqrt(TOTAL / norm)
    res[8:16, :] = jnp.where(keep, jnp.concatenate([rot, new], axis=1), -slope)
    for copy in last:
        copy.wait_send()


def finish_kernel(res, forces, rot_out, mode_out, curv):
    curv[...] = res[11:12, 0:128]
    for i in range(3):
        forces[i] = res[i:i + 1, :]
        rot_out[i] = res[8 + i:9 + i, 0:H]
        mode_out[i] = res[8 + i:9 + i, H:A]


def local(positions, mode, features, neighbours, counts, send_index, w_filter_in, b_filter, w_filter_out,
          w_project, w_update_in, b_update, w_update_out, w_readout, w_energy):
    vm = pl.BlockSpec(memory_space=pltpu.VMEM)
    hbm = pl.BlockSpec(memory_space=pltpu.HBM)
    S = jax.ShapeDtypeStruct

    def V(*s, dt=f32):
        return pltpu.VMEM(s, dt)

    dma = pltpu.SemaphoreType.DMA
    reds = [V(1, 1, 128), V(G1, 1, 128), V(1, 1, 128), V(G2, 1, 128)]
    sems = [dma((G1,)), dma((G1,)), dma((G2,)), dma((G2,))]
    args = (
        positions, mode, features, neighbours, counts.reshape(1, 1), send_index, w_filter_in, b_filter[None], w_filter_out,
        w_project, w_update_in, b_update[None], w_update_out, w_readout, w_energy[None])
    res = pl.pallas_call(
        main_kernel, out_shape=S((16, A), f32),
        in_specs=[hbm] * 15, out_specs=vm,
        scratch_shapes=[pltpu.VMEM(v.shape, v.dtype) for v in args] + [dma((15,))] + scratch()
        + reds + reds + [dma((2,))] * 2 + [dma((4,))] * 2 + [dma((1,))] * 2 + sems + sems,
        compiler_params=pltpu.CompilerParams(collective_id=0, has_side_effects=True),
    )(*args)
    forces, rot, new_mode, curv = pl.pallas_call(
        finish_kernel, out_shape=(S((3, 1, A), f32), S((3, 1, H), f32), S((3, 1, H), f32), S((1, 128), f32)),
        in_specs=[vm], out_specs=(vm, vm, vm, vm), compiler_params=pltpu.CompilerParams(vmem_limit_bytes=4 << 20),
    )(res)
    return (forces.transpose(1, 0, 2), rot, new_mode, curv[0, 0:1])


def solution(mesh):
    col = P(None, "dom")
    in_specs = (col, col, col, col, P("dom"), col) + (P(),) * 9
    out_specs = (P("image", None, "dom"), P(None, "image", "dom"), P(None, "image", "dom"), P())
    return jax.shard_map(local, mesh=mesh, in_specs=in_specs, out_specs=out_specs, check_vma=False)
```

```python
import functools

import jax
import jax.numpy as jnp
from jax import lax
from jax.experimental import pallas as pl
from jax.experimental.pallas import tpu as pltpu
from jax.sharding import PartitionSpec as P

f32 = jnp.float32
bf = jnp.bfloat16
CH = 64
RBF = 32
NBR = 12
A = 1024
H = 512
LO = 256
STEP = 0.05
TURN = 0.5
X, Y, Z = 4, 4, 8
G1, G2 = X * Y, Z
DOM = X * Y * Z
TOTAL = 3.0 * DOM * A
MESH = pl.DeviceIdType.MESH


def split(x):
    hi = x.astype(bf)
    return hi, (x - hi.astype(f32)).astype(bf)

def wcat(w):
    hi, lo = split(w)
    return jnp.concatenate([hi, lo, hi], axis=1)

def dot3(wc, x):
    hi, lo = split(x)
    return jnp.dot(wc, jnp.concatenate([hi, hi, lo], axis=0), preferred_element_type=f32)

def column(row_ref):
    return jnp.broadcast_to(row_ref[...], (128, row_ref.shape[1])).T

def tiled(col, L):
    return jnp.concatenate([col] * (L // 128), axis=1)

def sig(x):
    return 0.5 * jnp.tanh(0.5 * x) + 0.5

def stage_c(summed, feat, cnt, wui, wuit, wuo, wuot, wr, wrt, bucol, wecol, L=1024):
    for l in range(0, A, L):
        pre = dot3(wuit[...], summed[:, l:l+L]) + tiled(bucol[...], L)
        s = sig(pre)
        inner = pre * s
        upd = feat[:, l:l+L] + dot3(wuot[...], inner)
        r = dot3(wrt[...], upd)
        sr = sig(r)
        valid = lax.broadcasted_iota(jnp.int32, (CH, L), 1) + l < cnt
        dr = jnp.where(valid, tiled(wecol[...], L) * (sr + r * sr * (1.0 - sr)), 0.0)
        du = dot3(wr[...], dr)
        di = dot3(wuo[...], du)
        dp = di * (s + inner * (1.0 - s))
        summed[:, l:l+L] = dot3(wui[...], dp)

def back_slope(k, slopes, od, dsum, own):
    dd = jnp.sum(dsum[...] * slopes[k], axis=0, keepdims=True)
    D = od[k] * dd
    own[...] -= D
    Dh = D.astype(bf).astype(f32)
    return Dh + pltpu.roll(D - Dh, 3, axis=0)


def back_scatter(k, nbr, onehot, D8, first):
    hib = jnp.broadcast_to(nbr[pl.ds(k, 1), :] >> 7, (8, A))
    Gm = jnp.concatenate([jnp.where(hib == first + h, D8, 0.0) for h in range(8)], axis=0).astype(bf)
    O = onehot[k, 0:128, :] + onehot[k, 128:256, :]
    return lax.dot_general(Gm, O, (((1,), (1,)), ((), ())), preferred_element_type=f32)


class Place:
    def __init__(self):
        self.image = lax.axis_index("image")
        self.dom = lax.axis_index("dom")
        self.x = self.dom % X
        self.z = (self.dom // X) % Z
        self.y = self.dom // (X * Z)
        self.slot1 = self.y * X + self.x
        self.up = (self.image, (self.dom + 1) % DOM)
        self.down = (self.image, (self.dom + DOM - 1) % DOM)
        self.up2 = (1 - self.image, self.up[1])
        self.down2 = (1 - self.image, self.down[1])
        self.partner = (1 - self.image, self.dom)

    def peer1(self, o):
        y, x = (self.y + o // X) % Y, (self.x + o % X) % X
        return (self.image, y * (X * Z) + self.z * X + x), y * X + x

    def peer2(self, o):
        z = (self.z + o) % Z
        return (self.image, self.y * (X * Z) + z * X + self.x), z


def hops(o, n):
    return min(o, n - o)


ORDER1 = sorted(range(1, G1), key=lambda o: -hops(o // X, Y) - hops(o % X, X))
ORDER2 = sorted(range(1, G2), key=lambda o: -hops(o, Z))


def greet(pos, extra):
    barrier = pltpu.get_barrier_semaphore()
    peers = [pos.peer2(o)[0] for o in ORDER2] + [pos.peer1(o)[0] for o in ORDER1] + extra
    for peer in peers:
        pl.semaphore_signal(barrier, inc=1, device_id=peer, device_id_type=MESH)
    return barrier, len(peers)


def spread(src, dst, slot, order, peer_of, ssem, rsem):
    copies = []
    for o in order:
        copy = pltpu.make_async_remote_copy(
            src_ref=src.at[0], dst_ref=dst.at[slot], send_sem=ssem.at[o], recv_sem=rsem.at[slot],
            device_id=peer_of(o)[0], device_id_type=MESH)
        copy.start()
        copies.append(copy)
    return copies


def gather_wait(dst, order, rsem, src, ssem, peer_of):
    for o in reversed(order):
        device, other = peer_of(o)
        pltpu.make_async_remote_copy(
            src_ref=src.at[0], dst_ref=dst.at[other], send_sem=ssem.at[o], recv_sem=rsem.at[other],
            device_id=device, device_id_type=MESH).wait_recv()


LANE_ROWS = 24
MM = CH - LANE_ROWS


def select_blocks(hi, G, blocks, first, L, acc=None):
    hib = jnp.broadcast_to(hi, (MM, L))
    for h in range(blocks):
        block = G[h * MM:h * MM + MM]
        acc = jnp.where(hib == first + h, block, jnp.zeros((MM, L), f32) if acc is None else acc)
    return acc


def one_hot(lo, L):
    rows = lax.broadcasted_iota(jnp.int32, (LO, L), 0).astype(f32).astype(bf)
    at = jnp.broadcast_to(lo.astype(f32), (LO, L)).astype(bf)
    return jnp.where(rows == at, jnp.ones((), bf), jnp.zeros((), bf))


def pick_rows(table, idx, groups, first=0, acc=None, at=0, rows=8):
    lo = jnp.broadcast_to(idx & 127, (8, 128))
    hi = jnp.broadcast_to(idx >> 7, (8, 128))
    out = []
    for r in range(0, rows, 8):
        v = jnp.zeros((8, 128), f32) if acc is None else acc[r:r + 8]
        for h in range(groups):
            c = at + h * 128
            got = jnp.take_along_axis(table[r:r + 8, c:c + 128], lo, axis=1)
            v = jnp.where(hi == first + h, got, v)
        out.append(v)
    return jnp.concatenate(out, axis=0) if len(out) > 1 else out[0]


def set_tab(tab, h, proj):
    at = (h // 4) * (8 * MM) + (h % 4) * MM
    hi, lo = split(proj)
    tab[at:at + MM, :] = hi
    tab[at + 4 * MM:at + 5 * MM, :] = lo


def look_up(table, O):
    G = jnp.dot(table, O, preferred_element_type=f32)
    return G[0:4 * MM] + G[4 * MM:8 * MM]


def stage_own(k, nbr, tab, lanes, onehot, pt, L=256):
    row = nbr[pl.ds(k, 1), :]
    for l in range(0, A, L):
        idx = row[:, l:l + L]
        O = one_hot(idx & (LO - 1), L)
        onehot[k, :, l:l + L] = O
        pt[k, LANE_ROWS:CH, l:l + L] = select_blocks(idx >> 8, look_up(tab[0:8 * MM, :], O), 4, 0, L)
        for m in range(l, l + L, 128):
            if LANE_ROWS:
                pt[k, 0:LANE_ROWS, m:m + 128] = pick_rows(lanes, row[:, m:m + 128], 8, rows=LANE_ROWS)


def stage_rim(k, nbr, tab, lanes, onehot, pt, gt, L=256):
    row = nbr[pl.ds(k, 1), :]
    for l in range(0, A, L):
        idx = row[:, l:l + L]
        O = onehot[k, :, l:l + L]
        gt[k, LANE_ROWS:CH, l:l + L] = select_blocks(
            idx >> 8, look_up(tab[8 * MM:16 * MM, :], O), 4, 4, L, pt[k, LANE_ROWS:CH, l:l + L])
        for m in range(l, l + L, 128):
            if LANE_ROWS:
                gt[k, 0:LANE_ROWS, m:m + 128] = pick_rows(
                    lanes, row[:, m:m + 128], 8, 8, pt[k, 0:LANE_ROWS, m:m + 128], A, LANE_ROWS)


SHARP = 0.25 * ((RBF - 1) / 2.5) ** 2


def pick_position(pos8, idx):
    wide = jnp.broadcast_to(idx, (8, 128))
    lo = wide & 127
    bit = [(wide & (128 << i)) != 0 for i in range(4)]
    v = [jnp.take_along_axis(pos8[:, h * 128:h * 128 + 128], lo, axis=1) for h in range(8)]
    for i in range(3):
        v = [jnp.where(bit[i], v[j + 1], v[j]) for j in range(0, len(v), 2)]
    return jnp.where(bit[3], pltpu.roll(v[0], 4, axis=0), v[0])


def pair_distance(k, nbr, pos8, od, dist, L=256):
    row = nbr[pl.ds(k, 1), :]
    keep = lax.broadcasted_iota(jnp.int32, (8, L), 0) < 3
    for l in range(0, A, L):
        there = jnp.concatenate([pick_position(pos8, row[:, m:m + 128]) for m in range(l, l + L, 128)], axis=1)
        off = jnp.where(keep, there - pos8[:, l:l + L], 0.0)
        d = jnp.sqrt(jnp.sum(off * off, axis=0, keepdims=True) + 0.01)
        od[k, :, l:l + L] = off / d
        dist[:, l:l + L] = jnp.broadcast_to(d, (8, L))


def pair_filter(w1, bcol, dist, hz, L=256):
    bl = tiled(bcol[...], L)
    cen = lax.broadcasted_iota(jnp.int32, (RBF, L), 0).astype(f32) * 2.5 / (RBF - 1)
    for l in range(0, A, L):
        t = jnp.concatenate([dist[:, l:l + L]] * (RBF // 8), axis=0) - cen
        basis = jnp.exp(-SHARP * (t * t))
        pq = dot3(w1[...], jnp.concatenate([basis, basis * ((-2.0 * SHARP) * t)], axis=1))
        pre = pq[:, :L] + bl
        s = sig(pre)
        hdn = pre * s
        z = (s + hdn * (1.0 - s)) * pq[:, L:]
        for at, v in ((l, hdn), (A + l, z)):
            hi, lo = split(v)
            hz[0:64, at:at + L] = hi
            hz[64:128, at:at + L] = lo


def pair_apply(k, w2, hz, gt, slopes, summed, L=256):
    for l in range(0, A, L):
        both = []
        for at in (l, A + l):
            hi, lo = hz[0:64, at:at + L], hz[64:128, at:at + L]
            both.append(jnp.dot(w2[...], jnp.concatenate([hi, hi, lo], axis=0), preferred_element_type=f32))
        g = gt[k, :, l:l + L]
        summed[:, l:l + L] += both[0] * g
        slopes[k, :, l:l + L] = both[1] * g


def total(v):
    return jnp.sum(jnp.sum(v, axis=1, keepdims=True), axis=0, keepdims=True)


def ratio(p, m):
    return jnp.where(m > 0.0, p / jnp.where(m > 0.0, m, 1.0), 0.0)


def row_of(p, m, r):
    lane = lax.broadcasted_iota(jnp.int32, (1, 128), 1)
    return jnp.where(lane == 0, p, jnp.where(lane == 1, m, r))


def merge(ref):
    rows = ref[:, 0, :]
    p, m, r = rows[:, 0:1], rows[:, 1:2], rows[:, 2:3]
    sums = [jnp.sum(v, axis=0, keepdims=True) for v in (p, m, r)]
    return sums, ratio(p, m), m


SCR_NAMES = (
    "tab", "lanes", "pm", "rim", "left", "right", "pos8", "onehot", "pickhot", "pt", "gt", "slopes", "hz", "dist",
    "summed", "od", "d8", "own", "sc", "back", "extra", "mine", "theirs", "unit",
    "w1", "w2", "bcol", "bucol", "wecol", "wui", "wuit", "wuo", "wuot", "wr", "wrt")


def scratch():
    def V(*s, dt=f32):
        return pltpu.VMEM(s, dt)

    return [
        V(16 * MM, LO, dt=bf), V(max(LANE_ROWS, 8), 2 * A), V(8, A), V(2, 72, H), V(72, H), V(72, H), V(8, A),
        V(NBR, LO, A, dt=bf), V(128, A, dt=bf), V(NBR, CH, A), V(NBR, CH, A), V(NBR, CH, A),
        V(2 * CH, 2 * A, dt=bf), V(8, A), V(CH, A), V(NBR, 8, A), V(NBR, 8, A), V(8, A), V(128, 128),
        V(2, 8, H), V(2, 2, 8, H), V(8, A), V(8, A), V(8, A),
        V(64, 96, dt=bf), V(64, 192, dt=bf), V(64, 128), V(64, 128), V(64, 128)] + [V(64, 192, dt=bf)] * 6


def prep(sd, wfi, bf_, wfo, wui_, bu, wuo_, wr_, we):
    sd["w1"][...] = wcat(wfi[...].T)
    sd["bcol"][...] = column(bf_)
    sd["w2"][...] = wcat(wfo[...].T)
    for name, ref in (("wui", wui_), ("wuo", wuo_), ("wr", wr_)):
        sd[name][...] = wcat(ref[...])
        sd[name + "t"][...] = wcat(ref[...].T)
    sd["bucol"][...] = column(bu)
    sd["wecol"][...] = column(we)
    for name in ("summed", "own", "sc"):
        sd[name][...] = jnp.zeros_like(sd[name])


LOOK_UNROLL = 6


def run_own(sd, nbr):
    def body(i, c):
        for j in range(LOOK_UNROLL):
            stage_own(i * LOOK_UNROLL + j, nbr, sd["tab"], sd["lanes"], sd["onehot"], sd["pt"])
        return c

    lax.fori_loop(0, NBR // LOOK_UNROLL, body, 0)


def run_rim(sd, nbr):
    def body(i, c):
        for j in range(LOOK_UNROLL):
            stage_rim(i * LOOK_UNROLL + j, nbr, sd["tab"], sd["lanes"], sd["onehot"], sd["pt"], sd["gt"])
        return c

    lax.fori_loop(0, NBR // LOOK_UNROLL, body, 0)


def run_pair(sd, nbr):
    def distance(k):
        pair_distance(k, nbr, sd["pos8"], sd["od"], sd["dist"])

    def hidden():
        pair_filter(sd["w1"], sd["bcol"], sd["dist"], sd["hz"])

    def apply(k):
        pair_apply(k, sd["w2"], sd["hz"], sd["gt"], sd["slopes"], sd["summed"])

    def body(k, c):
        apply(k - 2)
        hidden()
        distance(k)
        return c

    distance(0)
    hidden()
    distance(1)
    lax.fori_loop(2, NBR, body, 0)
    apply(NBR - 2)
    hidden()
    apply(NBR - 1)


def run_update(sd, feat, cnt):
    stage_c(sd["summed"], feat, cnt, sd["wui"], sd["wuit"], sd["wuo"], sd["wuot"], sd["wr"], sd["wrt"],
            sd["bucol"], sd["wecol"])


BACK_UNROLL = 6


def run_back(sd, nbr, part):
    def body(i, c):
        acc = sd["sc"][64 * part:64 * part + 64, :]
        for j in range(BACK_UNROLL):
            k = i * BACK_UNROLL + j
            if part:
                D8 = back_slope(k, sd["slopes"], sd["od"], sd["summed"], sd["own"])
                sd["d8"][k] = D8
            else:
                D8 = sd["d8"][k]
            acc = acc + back_scatter(k, nbr, sd["onehot"], D8, 8 * part)
        sd["sc"][64 * part:64 * part + 64, :] = acc
        return c

    lax.fori_loop(0, NBR // BACK_UNROLL, body, 0)


def grad_block(sd, h):
    v = jnp.concatenate([sd["sc"][16 * h:16 * h + 8, :], sd["sc"][16 * h + 8:16 * h + 16, :]], axis=1)
    v = v + pltpu.roll(v, 5, axis=0)
    return v + sd["own"][:, h * LO:(h + 1) * LO] if h < 4 else v


def push(src, dst, send_sem, recv_sem, peer):
    copy = pltpu.make_async_remote_copy(
        src_ref=src, dst_ref=dst, send_sem=send_sem, recv_sem=recv_sem, device_id=peer, device_id_type=MESH)
    copy.start()
    return copy


LOAD_ORDER = (1, 4, 0, 9, 2, 5, 3, 6, 7, 8, 10, 11, 12, 13, 14)


def main_kernel(*refs):
    inputs, res, held, load_sem, scr = refs[:15], refs[15], refs[16:31], refs[31], refs[32:]
    loads = [pltpu.make_async_copy(inputs[i], held[i], load_sem.at[i]) for i in range(15)]
    for i in LOAD_ORDER:
        loads[i].start()
    pos_ref, mode_ref, feat, nbr, cnt_ref, send_ref, wfi, bf_, wfo, wp_ref, wui_, bu, wuo_, wr_, we = held
    sd = dict(zip(SCR_NAMES, scr))
    tab, lanes, pm, rim, left, right, pos8 = [sd[n] for n in ("tab", "lanes", "pm", "rim", "left", "right", "pos8")]
    pickhot, own, back, extra = [sd[n] for n in ("pickhot", "own", "back", "extra")]
    mine, theirs, unit = [sd[n] for n in ("mine", "theirs", "unit")]
    (a1s, a1, a2s, a2, b1s, b1, b2s, b2, hs, hr, gs, gr, xs, xr,
     sa1, ra1, sa2, ra2, sb1, rb1, sb2, rb2) = scr[len(SCR_NAMES):]
    pos = Place()
    barrier, count = greet(pos, [pos.up, pos.down, pos.partner, pos.up2, pos.down2])
    for i in LOAD_ORDER[:3]:
        loads[i].wait()
    cnt = jnp.broadcast_to(cnt_ref[...], (8, 128))
    valid = lax.broadcasted_iota(jnp.int32, (3, A), 1) < cnt[0:1, 0:1]
    masked = jnp.where(valid, mode_ref[...], 0.0)
    part = jnp.broadcast_to(total(masked * masked), (1, 128))
    a1s[0] = part
    a1[pl.ds(pos.slot1, 1)] = part[None]
    pm[...] = jnp.concatenate([pos_ref[...], masked, jnp.zeros((2, A), f32)], axis=0)
    for i in LOAD_ORDER[3:6]:
        loads[i].wait()
    wpt = wcat(wp_ref[...].T)
    for h in range(4):
        proj = dot3(wpt, feat[:, h * LO:(h + 1) * LO])
        lanes[:, h * LO:(h + 1) * LO] = proj[0:LANE_ROWS]
        set_tab(tab, h, proj[LANE_ROWS:])
    for side in range(2):
        row = send_ref[side:side + 1, :]
        for l in range(0, H, 256):
            idx = row[:, l:l + 256]
            O = one_hot(idx & (LO - 1), 256)
            pickhot[:, side * H + l:side * H + l + 256] = O[0:128] + O[128:256]
            rim[side, LANE_ROWS:CH, l:l + 256] = select_blocks(idx >> 8, look_up(tab[0:8 * MM, :], O), 4, 0, 256)
        for l in range(0, H, 128):
            rim[side, 0:LANE_ROWS, l:l + 128] = pick_rows(lanes, row[:, l:l + 128], 8, rows=LANE_ROWS)
            rim[side, CH:CH + 8, l:l + 128] = pick_rows(pm, row[:, l:l + 128], 8)
    for i in LOAD_ORDER[6:]:
        loads[i].wait()
    prep(sd, wfi, bf_, wfo, wui_, bu, wuo_, wr_, we)
    pl.semaphore_wait(barrier, count)
    sent = spread(a1s, a1, pos.slot1, ORDER1, pos.peer1, sa1, ra1)
    low = push(rim.at[0], right, hs.at[0], hr.at[0], pos.down)
    high = push(rim.at[1], left, hs.at[1], hr.at[1], pos.up)
    sent += [low, high]

    run_own(sd, nbr)
    gather_wait(a1, ORDER1, ra1, a1s, sa1, pos.peer1)
    part = jnp.sum(a1[:, 0, :], axis=0, keepdims=True)
    a2s[0] = part
    a2[pl.ds(pos.z, 1)] = part[None]
    sent += spread(a2s, a2, pos.z, ORDER2, pos.peer2, sa2, ra2)
    low.wait_recv()
    high.wait_recv()
    for buf, at in ((left, 4), (right, 6)):
        lanes[:, at * LO:(at + 2) * LO] = buf[0:LANE_ROWS, :]
        for h in range(2):
            set_tab(tab, at + h, buf[LANE_ROWS:CH, h * LO:(h + 1) * LO])
    run_rim(sd, nbr)
    gather_wait(a2, ORDER2, ra2, a2s, sa2, pos.peer2)
    part = jnp.sum(a2[:, 0, :], axis=0, keepdims=True)
    scale = jnp.sqrt(TOTAL / part[:, 0:1])
    sign = 1.0 - 2.0 * pos.image.astype(f32)
    moves = sign * STEP
    u = pm[3:6, :] * scale
    unit[...] = jnp.concatenate([u, jnp.zeros((5, A), f32)], axis=0)
    shift = jnp.where(lax.broadcasted_iota(jnp.int32, (3, H), 0) == 0, 1.0, 0.0)
    sides = [buf[CH:CH + 3, :] + moves * (buf[CH + 3:CH + 6, :] * scale) for buf in (left, right)]
    beside = jnp.concatenate([sides[0] - shift, sides[1] + shift], axis=1)
    gap = jnp.zeros((1, A), f32)
    pos8[...] = jnp.concatenate([pm[0:3, :] + moves * u, gap, beside, gap], axis=0)

    run_pair(sd, nbr)
    run_update(sd, feat, cnt[0:1, 0:1])
    run_back(sd, nbr, 1)

    keep = lax.broadcasted_iota(jnp.int32, (8, A), 0) < 3
    for h in range(4, 8):
        back[(h - 4) // 2, :, (h % 2) * LO:(h % 2 + 1) * LO] = grad_block(sd, h)
    moved = [push(back.at[1], extra.at[0, 0], gs.at[0], gr.at[0], pos.up),
             push(back.at[0], extra.at[0, 1], gs.at[1], gr.at[1], pos.down),
             push(back.at[1], extra.at[1, 0], gs.at[2], gr.at[2], pos.up2),
             push(back.at[0], extra.at[1, 1], gs.at[3], gr.at[3], pos.down2)]
    run_back(sd, nbr, 0)
    for h in range(4):
        mine[:, h * LO:(h + 1) * LO] = jnp.where(keep[:, 0:LO], grad_block(sd, h), 0.0)
    moved += [push(mine, theirs, xs.at[0], xr.at[0], pos.partner)]
    for copy in sent:
        copy.wait_send()
    sent = moved
    u = unit[...]
    m = total(u * u)
    row = jnp.concatenate([send_ref[0:1, :], send_ref[1:2, :]], axis=1)
    hib = jnp.broadcast_to(row >> 7, (8, A))
    masks = [hib == h for h in range(8)]
    for copy in moved:
        copy.wait_recv()
    halves = []
    for i in range(2):
        D = jnp.where(keep, jnp.concatenate([extra[i, 0], extra[i, 1]], axis=1), 0.0)
        Dh = D.astype(bf).astype(f32)
        D8 = Dh + pltpu.roll(D - Dh, 3, axis=0)
        halves += [jnp.where(mask, D8, 0.0) for mask in masks]
    Gm = jnp.concatenate(halves, axis=0).astype(bf)
    S = lax.dot_general(Gm, pickhot[...], (((1,), (1,)), ((), ())), preferred_element_type=f32)
    force = []
    for i, ref in ((0, mine), (1, theirs)):
        v = jnp.concatenate([S[64 * i + 8 * h:64 * i + 8 * h + 8, :] for h in range(8)], axis=1)
        v = v + pltpu.roll(v, 5, axis=0)
        force.append(jnp.where(keep, -(ref[...] + v), 0.0))
    res[0:8, :] = force[0]
    diff = (sign / (2.0 * STEP)) * (force[0] - force[1])

    p = total(diff * u)
    rest = diff - ratio(p, m) * u
    packed = row_of(p, m, total(rest * rest))
    b1s[0] = packed
    b1[pl.ds(pos.slot1, 1)] = packed[None]
    sent += spread(b1s, b1, pos.slot1, ORDER1, pos.peer1, sb1, rb1)
    gather_wait(b1, ORDER1, rb1, b1s, sb1, pos.peer1)
    (p, m, r), qs, ms = merge(b1)
    away = qs - ratio(p, m)
    packed = row_of(p, m, r + jnp.sum(away * away * ms, axis=0, keepdims=True))
    b2s[0] = packed
    b2[pl.ds(pos.z, 1)] = packed[None]
    last = spread(b2s, b2, pos.z, ORDER2, pos.peer2, sb2, rb2)
    for copy in sent:
        copy.wait_send()
    gather_wait(b2, ORDER2, rb2, b2s, sb2, pos.peer2)
    (p, m, r), qs, ms = merge(b2)
    slope = p / TOTAL
    along = 1.0 + TURN * (qs - slope)
    norm = (TURN * TURN) * r + jnp.sum(along * along * ms, axis=0, keepdims=True)
    first = pos.image == 0
    uh = jnp.where(first, u[:, 0:H], u[:, H:A])
    rot = jnp.where(first, diff[:, 0:H], diff[:, H:A]) - slope * uh
    new = (uh + TURN * rot) * jnp.sqrt(TOTAL / norm)
    res[8:16, :] = jnp.where(keep, jnp.concatenate([rot, new], axis=1), -slope)
    for copy in last:
        copy.wait_send()


def finish_kernel(res, forces, rot_out, mode_out, curv):
    curv[...] = res[11:12, 0:128]
    for i in range(3):
        forces[i] = res[i:i + 1, :]
        rot_out[i] = res[8 + i:9 + i, 0:H]
        mode_out[i] = res[8 + i:9 + i, H:A]


def local(positions, mode, features, neighbours, counts, send_index, w_filter_in, b_filter, w_filter_out,
          w_project, w_update_in, b_update, w_update_out, w_readout, w_energy):
    vm = pl.BlockSpec(memory_space=pltpu.VMEM)
    hbm = pl.BlockSpec(memory_space=pltpu.HBM)
    S = jax.ShapeDtypeStruct

    def V(*s, dt=f32):
        return pltpu.VMEM(s, dt)

    dma = pltpu.SemaphoreType.DMA
    reds = [V(1, 1, 128), V(G1, 1, 128), V(1, 1, 128), V(G2, 1, 128)]
    sems = [dma((G1,)), dma((G1,)), dma((G2,)), dma((G2,))]
    args = (
        positions, mode, features, neighbours, counts.reshape(1, 1), send_index, w_filter_in, b_filter[None], w_filter_out,
        w_project, w_update_in, b_update[None], w_update_out, w_readout, w_energy[None])
    res = pl.pallas_call(
        main_kernel, out_shape=S((16, A), f32),
        in_specs=[hbm] * 15, out_specs=vm,
        scratch_shapes=[pltpu.VMEM(v.shape, v.dtype) for v in args] + [dma((15,))] + scratch()
        + reds + reds + [dma((2,))] * 2 + [dma((4,))] * 2 + [dma((1,))] * 2 + sems + sems,
        compiler_params=pltpu.CompilerParams(collective_id=0, has_side_effects=True),
    )(*args)
    forces, rot, new_mode, curv = pl.pallas_call(
        finish_kernel, out_shape=(S((3, 1, A), f32), S((3, 1, H), f32), S((3, 1, H), f32), S((1, 128), f32)),
        in_specs=[vm], out_specs=(vm, vm, vm, vm), compiler_params=pltpu.CompilerParams(vmem_limit_bytes=4 << 20),
    )(res)
    return (forces.transpose(1, 0, 2), rot, new_mode, curv[0, 0:1])


def solution(mesh):
    col = P(None, "dom")
    in_specs = (col, col, col, col, P("dom"), col) + (P(),) * 9
    out_specs = (P("image", None, "dom"), P(None, "image", "dom"), P(None, "image", "dom"), P())
    return jax.shard_map(local, mesh=mesh, in_specs=in_specs, out_specs=out_specs, check_vma=False)
```
